256 devices in a mesh: dp: 32 (over y, z_hi, core), centre: 8 (over x, z_lo).
Axes of the slice: x: 4, y: 4, z: 8 (z_hi: 4, z_lo: 2; z = z_hi * 2 + z_lo), core: 2. Of those that a mesh axis runs over, the one named last changes fastest.
Arguments:
- samples: float32 [16384, 512], P('dp'), may hold values from -4 to 4
- targets: float32 [16384, 64], P('dp'), may hold values from -6 to 6
- centres: float32 [32768, 512], P('centre'), may hold values from -4 to 4
- coefficients: float32 [32768, 64], P('centre'), may hold values from -0.9 to 0.9
Outputs:
- residual: float32 [16384, 64], P('dp')
- new_coefficients: float32 [32768, 64], P(('centre', 'dp'))
The draws below stay inside these ranges and needn't reach their ends.
All inputs are finite; a program needn't handle non-finite values.
Results may differ from the reference program's by a relative error of at most 0.0001.
Values sent between devices are 32-bit elements; how exact they have to be, the bound alone decides.
A program may use at most 128 MiB of HBM per device.

```python
import math
import jax
import jax.numpy as jnp
from jax import lax

D = 512
OUTS = 64
ITERS = 2
ROWS_DEV = 512
SUB = 128
N = 16384
W = 32768
N_CENTRE = 8


latent_rank = 4


floor_ratio = 0.9


latent_ratio = 0.354


def embedding(key):
    embed_key = jax.random.fold_in(key, 7)
    return jax.random.normal(embed_key, (latent_rank, D), jnp.float32) * float(D) ** (-0.5)


def geometry_scale():
    return 0.1 * math.log(float(W)) - 0.04


def manifold_points(key, total_rows, offset_tag):
    scale = geometry_scale()
    point_key = jax.random.fold_in(key, offset_tag)
    latent_key = jax.random.fold_in(point_key, 0)
    noise_key = jax.random.fold_in(point_key, 2)
    latent = jax.random.normal(latent_key, (total_rows, latent_rank), jnp.float32)
    latent = jnp.clip(latent, -6.0, 6.0) * (latent_ratio * scale)
    placed = jnp.dot(latent, embedding(key), precision=jax.lax.Precision.HIGHEST)
    noise = jax.random.normal(noise_key, (total_rows, D), jnp.float32) * (floor_ratio * scale / math.sqrt(2.0 * float(D)))
    return jnp.clip(placed + noise, -4.0, 4.0)


def draw_samples(key, part):
    return manifold_points(key, N, 11)


def draw_centres(key, part):
    return manifold_points(key, W, 13)


def levels(own_key, shape, cuts, smallest, high):
    gain, own = 1.0, jax.random.fold_in(own_key, 6)
    for axis_at, shards_of in cuts:
        steps = jnp.exp(jax.random.uniform(jax.random.fold_in(own, axis_at), (shards_of,), jnp.float32, smallest / len(cuts), high / len(cuts)))
        gain = gain * jnp.repeat(steps, shape[axis_at] // shards_of).reshape([-1 if axis == axis_at else 1 for axis in range(len(shape))])
    return gain


def gaussian(own_key, extent, deviation, bound, shards=(), dtype=jnp.bfloat16):
    loudness = levels(own_key, extent, shards, -0.22, 0.18) if shards else 1.0
    array = jax.random.normal(own_key, extent, jnp.float32) * deviation * loudness
    return jnp.minimum(jnp.maximum(array, -bound), bound).astype(dtype)


def setup_inputs(seed: int = 0) -> dict:
    streams_of = jax.random.split(jax.random.key(seed), 5)
    samples = draw_samples(jax.random.fold_in(streams_of[4], 71), 0)
    targets = gaussian(streams_of[1], (N, OUTS), 1.0, 6.0, ((0, 32),), jnp.float32)
    centres = draw_centres(jax.random.fold_in(streams_of[4], 71), 0)
    coefficients = gaussian(streams_of[3], (W, OUTS), 0.15, 0.9, ((0, 8),), jnp.float32)
    return {"samples": samples, "targets": targets, "centres": centres, "coefficients": coefficients}


softening = 0.01
kernel_scale = 0.2
learning_rate = 4.0

def kernel_block(left, right):
    cross = lax.dot_general(left, right, (((1,), (1,)), ((), ())), precision=lax.Precision.HIGHEST, preferred_element_type=jnp.float32)
    left_sq = lax.optimization_barrier(jnp.sum(left * left, axis=1))
    right_sq = lax.optimization_barrier(jnp.sum(right * right, axis=1))
    dist_sq = jnp.maximum(left_sq[:, None] + right_sq[None, :] - 2.0 * cross, 0.0)
    return jnp.exp(-jnp.sqrt(dist_sq + softening) / kernel_scale)

def matmul(left, right):
    return jnp.dot(left, right, precision=lax.Precision.HIGHEST, preferred_element_type=jnp.float32)

def reference(samples, targets, centres, coefficients):
    row_blocks = samples.reshape(-1, ROWS_DEV, D)
    predictions = lax.map(lambda block: matmul(kernel_block(block, centres), coefficients), row_blocks).reshape(-1, OUTS)
    residual = predictions - targets
    centre_blocks = centres.reshape(-1, SUB * N_CENTRE, D)
    gradient = lax.map(lambda block: matmul(kernel_block(block, samples), residual), centre_blocks).reshape(-1, OUTS)

    def first_pass(block):
        square = kernel_block(block, centres)
        return (lax.optimization_barrier(jnp.sum(square, axis=1)), matmul(square, gradient))
    row_sums, kernel_grad = lax.map(first_pass, centre_blocks)
    step_size = 1.0 / jnp.max(row_sums)
    theta = step_size * gradient
    image = step_size * kernel_grad.reshape(-1, OUTS)
    for turn in range(ITERS):
        if turn > 0:
            current = theta
            image = lax.map(lambda block: matmul(kernel_block(block, centres), current), centre_blocks).reshape(-1, OUTS)
        theta = theta + step_size * (gradient - image)
    return (residual, coefficients - learning_rate * theta)
```

```python
import functools
import math

import jax
import jax.numpy as jnp
from jax import lax
from jax.experimental import pallas as pl
from jax.experimental.pallas import tpu as pltpu
from jax.sharding import PartitionSpec as P

MESH = pl.DeviceIdType.MESH
f32, bf16 = jnp.float32, jnp.bfloat16
NT = (((1,), (1,)), ((), ()))

SOFTENING = 0.01
KERNEL_SCALE = 0.2
LEARNING_RATE = 4.0
SCALE_SQ = (math.log2(math.e) / KERNEL_SCALE) ** 2
EPS = SOFTENING * SCALE_SQ

PAIRS = ((0, 0), (0, 1), (1, 0), (3, 0), (1, 1), (3, 1), (2, 0), (2, 1))
PLACE = {pair: at for at, pair in enumerate(PAIRS)}
FIRST_ROWS = ((1, 0), (3, 0), (0, 1))
LATER_ROWS = ((2, 0), (2, 1), (1, 1), (3, 1))


def halves(x):
    hi = x.astype(bf16)
    lo = (x - hi.astype(f32)).astype(bf16)
    return hi, lo


def kernel_of(z):
    z = jnp.maximum(z, EPS)
    return jnp.exp2(-(z * lax.rsqrt(z)))


def lanes(x, times):
    return jnp.concatenate([x] * times, axis=1)


def step_kernel(
    samples, targets, centres, coefs, res_out, new_out,
    cen, cof, smp, tgt, rows,
    c3, ccol, crow, s3, scol, r3, rrow, cof2,
    kh, kl, th, tl,
    pacc, pred, pred_in, res, tgt_t, cof_t,
    gpart, g_y, gsum, g_z, gall,
    upart, u_core, usum, u_in, uall,
    vpart, v_core, vsum, v_in,
    lhs_r, lhs_u,
    loc_sem, smp_sem, row_send, row_recv, fwd_send, fwd_recv,
    p_send, p_recv, q_send, q_recv,
    gy_send, gy_recv, gz_send, gz_recv, az_send, az_recv, ay_send, ay_recv,
    uc_send, uc_recv, ur_send, ur_recv, bz_send, bz_recv, by_send, by_recv,
    vc_send, vc_recv, vr_send, vr_recv,
):
    d, c = lax.axis_index("dp"), lax.axis_index("centre")
    core, zh, y = d % 2, (d // 2) % 4, d // 8
    x, zl = c // 2, c % 2
    sib = d + 1 - 2 * core

    def at_y(j):
        return (((y + j) % 4 * 4 + zh) * 2 + core, c)

    def at_z(j):
        return ((y * 4 + (zh + j) % 4) * 2 + core, c)

    def centre_of(dx, dz):
        return (x + dx) % 4 * 2 + (zl + dz) % 2

    def remote(src, dst, send, recv, to):
        return pltpu.make_async_remote_copy(
            src_ref=src, dst_ref=dst, send_sem=send, recv_sem=recv, device_id=to, device_id_type=MESH
        )

    n = 128
    local = []

    def load(src, dst, sem):
        copy = pltpu.make_async_copy(src, dst, sem)
        copy.start()
        local.append(copy)
        return copy

    own_rows = pl.ds(pl.multiple_of(d * n, n), n)
    sib_rows = pl.ds(pl.multiple_of(sib * n, n), n)
    smp_load = load(samples, smp.at[0], loc_sem.at[0])
    cen_loads = []
    for b in range(16):
        owner = ((y + b // 4) % 4 * 4 + (zh + b % 4) % 4) * 2 + core
        at = pl.ds(pl.multiple_of(owner * n, n), n)
        cen_loads.append(load(centres.at[at], cen.at[pl.ds(b * n, n)], loc_sem.at[5 + b]))
    cof_loads = []
    for b in range(16):
        owner = ((y + b // 4) % 4 * 4 + (zh + b % 4) % 4) * 2 + core
        at = pl.ds(pl.multiple_of(owner * n, n), n)
        cof_loads.append(load(coefs.at[at], cof.at[pl.ds(b * n, n)], loc_sem.at[21 + b]))
    tgt_load = load(targets, tgt, loc_sem.at[1])
    row_loads = [
        load(centres.at[own_rows], rows.at[0, 0], loc_sem.at[2]),
        load(centres.at[sib_rows], rows.at[0, 1], loc_sem.at[3]),
    ]

    barrier = pltpu.get_barrier_semaphore()
    partners = [(sib, c)] + [at_y(j) for j in (1, 2, 3)] + [at_z(j) for j in (1, 2, 3)]
    for dx, dz in PAIRS[1:]:
        partners += [(d, centre_of(dx, dz)), (sib, centre_of(dx, dz))]
    for to in partners:
        pl.semaphore_signal(barrier, inc=1, device_id=to, device_id_type=MESH)
    pl.semaphore_wait(barrier, len(partners))

    sends = []
    smp_copy = remote(samples, smp.at[1], smp_sem.at[0], smp_sem.at[1], (sib, c))
    smp_copy.start()

    def send_rows(pairs):
        for dx, dz in pairs:
            j = PLACE[((4 - dx) % 4, dz)]
            copy = remote(
                centres.at[own_rows], rows.at[j, 0], row_send.at[PLACE[(dx, dz)]], row_recv.at[j], (d, centre_of(dx, dz))
            )
            copy.start()
            sends.append(copy)

    def forward_rows(j):
        remote(rows.at[j, 0], rows.at[j, 0], row_send.at[j], row_recv.at[j], (sib, c)).wait_recv()
        copy = remote(rows.at[j, 0], rows.at[j, 1], fwd_send.at[j], fwd_recv.at[j], (sib, c))
        copy.start()
        sends.append(copy)

    def await_forward(j):
        remote(rows.at[j, 0], rows.at[j, 1], fwd_send.at[j], fwd_recv.at[j], (sib, c)).wait_recv()

    send_rows(FIRST_ROWS)

    def norm_of(v):
        total = jnp.sum(v * v, axis=1, keepdims=True) * SCALE_SQ
        return jnp.broadcast_to(total, (n, n))

    def prepare_samples(half):
        def one(i, _):
            at = pl.ds(pl.multiple_of(i * n, n), n)
            to = pl.ds(pl.multiple_of(half * 512 + i * n, n), n)
            v = smp[half, at, :]
            hi, lo = halves(v * (-2.0 * SCALE_SQ))
            s3[to, 0:512] = hi
            s3[to, 512:1024] = hi
            s3[to, 1024:1536] = lo
            scol[to, :] = norm_of(v) + EPS
            return 0

        lax.fori_loop(0, 4, one, 0)

    def prepare_centres(i, _):
        at = pl.ds(pl.multiple_of(i * n, n), n)
        v = cen[at, :]
        hi, lo = halves(v)
        c3[at, 0:512] = hi
        c3[at, 512:1024] = lo
        c3[at, 1024:1536] = hi
        norms = norm_of(v)
        ccol[at, :] = norms + EPS
        crow[:, at] = norms.T[0:8, :]
        w = cof[at, :]
        whi = w.astype(bf16).astype(f32)
        cof2[at, :] = jnp.concatenate([whi, w - whi], axis=1).astype(bf16)
        return 0

    smp_load.wait()
    prepare_samples(0)
    for copy in cen_loads + cof_loads:
        copy.wait()
    lax.fori_loop(0, 16, prepare_centres, 0)
    smp_copy.wait_recv()
    prepare_samples(1)

    tn = 512
    pacc[...] = jnp.zeros_like(pacc)

    def data_tile(i, _):
        at = pl.ds(pl.multiple_of(i * tn, tn), tn)
        cross = lax.dot_general(s3[...], c3[at, :], NT, preferred_element_type=f32)
        value = kernel_of(cross + lanes(scol[...], tn // n) + crow[0:1, at])
        hi, lo = halves(value)
        kh[:, at] = hi
        kl[:, at] = lo
        w = cof2[at, :]
        pacc[...] += jnp.dot(hi, w, preferred_element_type=f32) + jnp.dot(lo, w, preferred_element_type=f32)
        return 0

    lax.fori_loop(0, 2048 // tn, data_tile, 0)
    both = pacc[...].T
    pred[...] = both[0:64] + both[64:128]

    group = [(dx, dz, kk) for dx, dz in PAIRS for kk in (0, 1)][1:]
    p_copies = []
    for s, (dx, dz, kk) in enumerate(group):
        to = centre_of(dx, dz)
        copy = remote(
            pred.at[pl.ds(pl.multiple_of(to * 8, 8), 8), pl.ds(kk * 512, 512)],
            pred_in.at[s], p_send.at[s], p_recv.at[s], (sib if kk else d, to),
        )
        copy.start()
        p_copies.append(copy)
    sends += p_copies

    tgt_load.wait()
    for copy in row_loads:
        copy.wait()
    wide = jnp.concatenate([tgt[...], jnp.zeros((512, 64), f32)], axis=1)
    tgt_t[...] = wide.T[0:64, :]
    wide = jnp.concatenate([cof[0:n, :], jnp.zeros((n, 64), f32)], axis=1)
    cof_t[...] = wide.T[0:64, :]

    tm = 512

    def square(j, _):
        for kk in (0, 1):
            v = rows[j, kk]
            hi, lo = halves(v * (-2.0 * SCALE_SQ))
            to = slice(kk * n, kk * n + n)
            r3[to, 0:512] = hi
            r3[to, 512:1024] = hi
            r3[to, 1024:1536] = lo
            rrow[:, to] = norm_of(v).T[0:8, :]
        cols = pl.ds(pl.multiple_of(j * 256, 256), 256)

        def tile(i, _):
            at = pl.ds(pl.multiple_of(i * tm, tm), tm)
            cross = lax.dot_general(c3[at, :], r3[...], NT, preferred_element_type=f32)
            hi, lo = halves(kernel_of(cross + lanes(ccol[at, :], 2) + rrow[0:1, :]))
            th[at, cols] = hi
            tl[at, cols] = lo
            return 0

        lax.fori_loop(0, 2048 // tm, tile, 0)
        return 0

    for pair in FIRST_ROWS:
        forward_rows(PLACE[pair])
    await_forward(PLACE[(0, 1)])
    lax.fori_loop(0, 2, square, 0)

    mine = pl.ds(pl.multiple_of(c * 8, 8), 8)
    for copy in p_copies:
        copy.wait_recv()
    total = pred[mine, 0:512] - tgt_t[mine, :]
    for s in range(15):
        total += pred_in[s]
    res[0, mine, :] = total
    q_copies = []
    for s, (dx, dz, kk) in enumerate(group):
        copy = remote(
            res.at[0, mine], res.at[kk, mine], q_send.at[s], q_recv.at[s], (sib if kk else d, centre_of(dx, dz))
        )
        copy.start()
        q_copies.append(copy)
    sends += q_copies
    await_forward(PLACE[(1, 0)])
    await_forward(PLACE[(3, 0)])
    lax.fori_loop(2, 4, square, 0)
    for copy in q_copies:
        copy.wait_recv()
    send_rows(LATER_ROWS)

    for kk in (0, 1):
        hi, lo = halves(res[kk])
        lhs_r[0:64, kk * 512 : kk * 512 + 512] = lo
        lhs_r[64:128, kk * 512 : kk * 512 + 512] = hi
    gy_copies = []
    for dy in (2, 1, 3, 0):
        at = slice(dy * 512, dy * 512 + 512)
        a = jnp.dot(lhs_r[...], kh[:, at], preferred_element_type=f32)
        b = jnp.dot(lhs_r[64:128, :], kl[:, at], preferred_element_type=f32)
        gpart[dy] = a[0:64] + a[64:128] + b
        if dy:
            copy = remote(gpart.at[dy], g_y.at[dy - 1], gy_send.at[dy - 1], gy_recv.at[dy - 1], at_y(dy))
            copy.start()
            gy_copies.append(copy)
    sends += gy_copies
    res_out[...] = res[0]
    for pair in LATER_ROWS:
        forward_rows(PLACE[pair])
    await_forward(4)
    lax.fori_loop(4, 5, square, 0)
    for copy in gy_copies:
        copy.wait_recv()
    gsum[...] = gpart[0] + g_y[0] + g_y[1] + g_y[2]
    gz_copies = []
    for dz in (2, 1, 3):
        copy = remote(
            gsum.at[:, pl.ds(dz * n, n)], g_z.at[dz - 1], gz_send.at[dz - 1], gz_recv.at[dz - 1], at_z(dz)
        )
        copy.start()
        gz_copies.append(copy)
    sends += gz_copies
    await_forward(5)
    lax.fori_loop(5, 6, square, 0)
    for copy in gz_copies:
        copy.wait_recv()
    gall[0, :, 0:n] = gsum[:, 0:n] + g_z[0] + g_z[1] + g_z[2]

    def spread_z(buf, send, recv):
        copies = []
        for dz in (2, 1, 3):
            to = (4 - dz) % 4
            copy = remote(
                buf.at[0, :, pl.ds(0, n)], buf.at[0, :, pl.ds(to * n, n)], send.at[dz - 1], recv.at[dz - 1], at_z(dz)
            )
            copy.start()
            copies.append(copy)
        sends.extend(copies)
        return copies

    def spread_y(buf, send, recv):
        copies = []
        for dy in (2, 1, 3):
            copy = remote(buf.at[0], buf.at[(4 - dy) % 4], send.at[dy - 1], recv.at[dy - 1], at_y(dy))
            copy.start()
            copies.append(copy)
        sends.extend(copies)
        return copies

    az_copies = spread_z(gall, az_send, az_recv)
    await_forward(6)
    lax.fori_loop(6, 7, square, 0)
    for copy in az_copies:
        copy.wait_recv()
    ay_copies = spread_y(gall, ay_send, ay_recv)
    await_forward(7)
    lax.fori_loop(7, 8, square, 0)
    for copy in ay_copies:
        copy.wait_recv()

    def project(buf, out, ones):
        for dy in range(4):
            hi, lo = halves(buf[dy, 0:64, :])
            lhs_u[0:64, dy * 512 : dy * 512 + 512] = lo
            lhs_u[64:128, dy * 512 : dy * 512 + 512] = hi
        if ones:
            lhs_u[128:144, :] = jnp.ones((16, 2048), bf16)
        top = 144 if ones else 128

        def tile(i, _):
            at = pl.ds(pl.multiple_of(i * 512, 512), 512)
            a = jnp.dot(lhs_u[0:top, :], th[:, at], preferred_element_type=f32)
            b = jnp.dot(lhs_u[64:top, :], tl[:, at], preferred_element_type=f32)
            out[0:64, at] = a[0:64] + a[64:128] + b[0:64]
            if ones:
                out[64:72, at] = a[128:136] + b[64:72]
            return 0

        lax.fori_loop(0, 4, tile, 0)

    def swap_core(part, arrived, send, recv):
        copies = []
        for j in range(8):
            copy = remote(part.at[:, pl.ds((2 * j + 1) * n, n)], arrived.at[j], send.at[j], recv.at[j], (sib, c))
            copy.start()
            copies.append(copy)
        sends.extend(copies)
        for copy in copies:
            copy.wait_recv()

    def to_owners(summed, arrived, send, recv):
        copies = []
        for j, (dx, dz) in enumerate(PAIRS):
            if j:
                copy = remote(
                    summed.at[j], arrived.at[j - 1], send.at[j - 1], recv.at[j - 1], (d, centre_of(dx, dz))
                )
                copy.start()
                copies.append(copy)
        sends.extend(copies)
        for copy in copies:
            copy.wait_recv()

    project(gall, upart, True)
    swap_core(upart, u_core, uc_send, uc_recv)
    for j in range(8):
        usum[j] = upart[:, 2 * j * n : 2 * j * n + n] + u_core[j]
    to_owners(usum, u_in, ur_send, ur_recv)
    total = usum[0]
    for s in range(7):
        total += u_in[s]
    uall[0, 0:64, 0:n] = total[0:64]
    uall[0, 64:72, 0:n] = jnp.broadcast_to(jnp.max(total[64:72], axis=1, keepdims=True), (8, n))

    for copy in spread_z(uall, bz_send, bz_recv):
        copy.wait_recv()
    for copy in spread_y(uall, by_send, by_recv):
        copy.wait_recv()

    project(uall, vpart, False)
    largest = uall[0, 64:72, 0:n]
    for dy in range(4):
        for dz in range(4):
            largest = jnp.maximum(largest, uall[dy, 64:72, dz * n : dz * n + n])
    for j in range(16):
        vpart[64:72, j * n : j * n + n] = largest
    swap_core(vpart, v_core, vc_send, vc_recv)
    for j in range(8):
        vsum[j, 0:64] = vpart[0:64, 2 * j * n : 2 * j * n + n] + v_core[j, 0:64]
        vsum[j, 64:72] = jnp.maximum(largest, v_core[j, 64:72])
    to_owners(vsum, v_in, vr_send, vr_recv)
    twice = vsum[0, 0:64]
    largest = vsum[0, 64:72]
    for s in range(7):
        twice += v_in[s, 0:64]
        largest = jnp.maximum(largest, v_in[s, 64:72])
    size = jnp.concatenate([1.0 / largest] * 8, axis=0)
    once, grad = uall[0, 0:64, 0:n], gall[0, :, 0:n]
    theta = size * (3.0 * grad - size * (3.0 * once - size * twice))
    new_out[...] = cof_t[...] - LEARNING_RATE * theta

    smp_copy.wait_send()
    for copy in sends:
        copy.wait_send()


def body(samples, targets, centres, coefficients):
    dma = pltpu.SemaphoreType.DMA
    vmem = pltpu.VMEM
    res_t, new_t = pl.pallas_call(
        step_kernel,
        out_shape=(jax.ShapeDtypeStruct((64, 512), f32), jax.ShapeDtypeStruct((64, 128), f32)),
        in_specs=[pl.BlockSpec(memory_space=pl.ANY)] * 4,
        out_specs=[pl.BlockSpec(memory_space=vmem)] * 2,
        scratch_shapes=[
            vmem((2048, 512), f32), vmem((2048, 64), f32), vmem((2, 512, 512), f32), vmem((512, 64), f32),
            vmem((8, 2, 128, 512), f32),
            vmem((2048, 1536), bf16), vmem((2048, 128), f32), vmem((8, 2048), f32),
            vmem((1024, 1536), bf16), vmem((1024, 128), f32), vmem((256, 1536), bf16), vmem((8, 256), f32),
            vmem((2048, 128), bf16),
            vmem((1024, 2048), bf16), vmem((1024, 2048), bf16), vmem((2048, 2048), bf16), vmem((2048, 2048), bf16),
            vmem((1024, 128), f32), vmem((64, 1024), f32), vmem((15, 8, 512), f32), vmem((2, 64, 512), f32),
            vmem((64, 512), f32), vmem((64, 128), f32),
            vmem((4, 64, 512), f32), vmem((3, 64, 512), f32), vmem((64, 512), f32), vmem((3, 64, 128), f32),
            vmem((4, 64, 512), f32),
            vmem((72, 2048), f32), vmem((8, 72, 128), f32), vmem((8, 72, 128), f32), vmem((7, 72, 128), f32),
            vmem((4, 72, 512), f32),
            vmem((72, 2048), f32), vmem((8, 72, 128), f32), vmem((8, 72, 128), f32), vmem((7, 72, 128), f32),
            vmem((128, 1024), bf16), vmem((144, 2048), bf16),
            dma((37,)), dma((2,)), dma((8,)), dma((8,)), dma((8,)), dma((8,)),
            dma((15,)), dma((15,)), dma((15,)), dma((15,)),
            dma((3,)), dma((3,)), dma((3,)), dma((3,)), dma((3,)), dma((3,)), dma((3,)), dma((3,)),
            dma((8,)), dma((8,)), dma((7,)), dma((7,)), dma((3,)), dma((3,)), dma((3,)), dma((3,)),
            dma((8,)), dma((8,)), dma((7,)), dma((7,)),
        ],
        compiler_params=pltpu.CompilerParams(
            collective_id=0, has_side_effects=True, vmem_limit_bytes=63 * 2**20
        ),
    )(samples, targets, centres, coefficients)
    return res_t.T, new_t.T


def solution(mesh):
    return jax.shard_map(
        body,
        mesh=mesh,
        in_specs=(P("dp", None), P("dp", None), P("centre", None), P("centre", None)),
        out_specs=(P("dp", None), P(("centre", "dp"), None)),
        check_vma=False,
    )
```

```python
import functools
import math

import jax
import jax.numpy as jnp
from jax import lax
from jax.experimental import pallas as pl
from jax.experimental.pallas import tpu as pltpu
from jax.sharding import PartitionSpec as P

MESH = pl.DeviceIdType.MESH
f32, bf16 = jnp.float32, jnp.bfloat16
NT = (((1,), (1,)), ((), ()))

SOFTENING = 0.01
KERNEL_SCALE = 0.2
LEARNING_RATE = 4.0
SCALE_SQ = (math.log2(math.e) / KERNEL_SCALE) ** 2
EPS = SOFTENING * SCALE_SQ

PAIRS = ((0, 0), (0, 1), (1, 0), (3, 0), (2, 0), (1, 1), (3, 1), (2, 1))
PLACE = {pair: at for at, pair in enumerate(PAIRS)}
FIRST_ROWS = ((1, 0), (3, 0), (0, 1))
LATER_ROWS = ((1, 1), (3, 1))


def halves(x):
    hi = x.astype(bf16)
    lo = (x - hi.astype(f32)).astype(bf16)
    return hi, lo


def kernel_of(z):
    z = jnp.maximum(z, EPS)
    return jnp.exp2(-(z * lax.rsqrt(z)))


def lanes(x, times):
    return jnp.concatenate([x] * times, axis=1)


def step_kernel(
    samples, targets, centres, coefs, res_out, new_out,
    cen, cof, smp, tgt, rows,
    c3, ccol, crow, s3, scol, r3, rrow, cof2,
    kh, kl, th, tl,
    pacc, pred, pred_in, res,
    gpart, g_y, gsum, g_z, gall,
    upart, u_core, usum, u_in, uall,
    vpart, v_core, vsum, v_in,
    lhs_r, lhs_u,
    loc_sem, smp_send, smp_recv, row_send, row_recv, fwd_send, fwd_recv, rel_send, rel_recv,
    p_send, p_recv, q_send, q_recv,
    gy_send, gy_recv, gz_send, gz_recv, az_send, az_recv, ay_send, ay_recv,
    uc_send, uc_recv, ur_send, ur_recv, bz_send, bz_recv, by_send, by_recv,
    vc_send, vc_recv, vr_send, vr_recv,
):
    d, c = lax.axis_index("dp"), lax.axis_index("centre")
    core, zh, y = d % 2, (d // 2) % 4, d // 8
    x, zl = c // 2, c % 2
    sib = d + 1 - 2 * core

    def at_y(j):
        return (((y + j) % 4 * 4 + zh) * 2 + core, c)

    def at_z(j):
        return ((y * 4 + (zh + j) % 4) * 2 + core, c)

    def centre_of(dx, dz):
        return (x + dx) % 4 * 2 + (zl + dz) % 2

    def remote(src, dst, send, recv, to):
        return pltpu.make_async_remote_copy(
            src_ref=src, dst_ref=dst, send_sem=send, recv_sem=recv, device_id=to, device_id_type=MESH
        )

    n = 128
    local = []

    def load(src, dst, sem):
        copy = pltpu.make_async_copy(src, dst, sem)
        copy.start()
        local.append(copy)
        return copy

    own_rows = pl.ds(pl.multiple_of(d * n, n), n)
    sib_rows = pl.ds(pl.multiple_of(sib * n, n), n)
    smp_load = load(samples, smp.at[0], loc_sem.at[0])
    cen_loads = []
    for b in range(16):
        owner = ((y + b // 4) % 4 * 4 + (zh + b % 4) % 4) * 2 + core
        at = pl.ds(pl.multiple_of(owner * n, n), n)
        cen_loads.append(load(centres.at[at], cen.at[pl.ds(b * n, n)], loc_sem.at[5 + b]))
    cof_loads = []
    for b in range(16):
        owner = ((y + b // 4) % 4 * 4 + (zh + b % 4) % 4) * 2 + core
        at = pl.ds(pl.multiple_of(owner * n, n), n)
        cof_loads.append(load(coefs.at[:, at], cof.at[:, pl.ds(b * n, n)], loc_sem.at[21 + b]))
    tgt_load = load(targets, tgt, loc_sem.at[1])
    row_loads = [
        load(centres.at[own_rows], rows.at[0, 0], loc_sem.at[2]),
        load(centres.at[sib_rows], rows.at[0, 1], loc_sem.at[3]),
    ]

    barrier = pltpu.get_barrier_semaphore()
    partners = [(sib, c)] + [at_y(j) for j in (1, 2, 3)] + [at_z(j) for j in (1, 2, 3)]
    for dx, dz in PAIRS[1:]:
        partners += [(d, centre_of(dx, dz)), (sib, centre_of(dx, dz))]
    for to in partners:
        pl.semaphore_signal(barrier, inc=1, device_id=to, device_id_type=MESH)
    pl.semaphore_wait(barrier, len(partners))

    sends = []
    smp_load.wait()
    smp_copies = []
    for i in range(4):
        at = pl.ds(i * n, n)
        copy = remote(smp.at[0, at], smp.at[1, at], smp_send.at[i], smp_recv.at[i], (sib, c))
        copy.start()
        smp_copies.append(copy)
    sends += smp_copies
    cen_loads[0].wait()

    def send_rows(pairs):
        for dx, dz in pairs:
            j = PLACE[((4 - dx) % 4, dz)]
            copy = remote(
                cen.at[pl.ds(0, n)], rows.at[j, 0], row_send.at[PLACE[(dx, dz)]], row_recv.at[j], (d, centre_of(dx, dz))
            )
            copy.start()
            sends.append(copy)

    def await_rows(j):
        remote(rows.at[j, 0], rows.at[j, 0], row_send.at[j], row_recv.at[j], (sib, c)).wait_recv()

    def relay_rows(dz):
        far = PLACE[(2, dz)]
        for i, (back, on) in enumerate(((1, 3), (3, 1))):
            part = pl.ds(i * 64, 64)
            copy = remote(
                rows.at[PLACE[(back, dz)], 0, part], rows.at[far, 0, part],
                rel_send.at[dz * 2 + i], rel_recv.at[dz * 2 + i], (d, centre_of(on, 0)),
            )
            copy.start()
            sends.append(copy)

    def await_relayed(dz):
        for i in (0, 1):
            part = rows.at[PLACE[(2, dz)], 0, pl.ds(i * 64, 64)]
            remote(part, part, rel_send.at[dz * 2 + i], rel_recv.at[dz * 2 + i], (sib, c)).wait_recv()

    def forward_rows(j):
        copy = remote(rows.at[j, 0], rows.at[j, 1], fwd_send.at[j], fwd_recv.at[j], (sib, c))
        copy.start()
        sends.append(copy)

    def await_forward(j):
        remote(rows.at[j, 0], rows.at[j, 1], fwd_send.at[j], fwd_recv.at[j], (sib, c)).wait_recv()

    send_rows(FIRST_ROWS)

    def norm_of(v):
        total = jnp.sum(v * v, axis=1, keepdims=True) * SCALE_SQ
        return jnp.broadcast_to(total, (n, n))

    def prepare_samples(half):
        def one(i, _):
            at = pl.ds(pl.multiple_of(i * n, n), n)
            to = pl.ds(pl.multiple_of(half * 512 + i * n, n), n)
            v = smp[half, at, :]
            hi, lo = halves(v * (-2.0 * SCALE_SQ))
            s3[to, 0:512] = hi
            s3[to, 512:1024] = hi
            s3[to, 1024:1536] = lo
            scol[to, :] = norm_of(v) + EPS
            return 0

        lax.fori_loop(0, 4, one, 0)

    def prepare_centres(i, _):
        at = pl.ds(pl.multiple_of(i * n, n), n)
        v = cen[at, :]
        hi, lo = halves(v)
        c3[at, 0:512] = hi
        c3[at, 512:1024] = lo
        c3[at, 1024:1536] = hi
        norms = norm_of(v)
        ccol[at, :] = norms + EPS
        crow[:, at] = norms.T[0:8, :]
        w = cof[:, at]
        whi = w.astype(bf16).astype(f32)
        cof2[at, :] = jnp.concatenate([whi, w - whi], axis=0).T.astype(bf16)
        return 0

    prepare_samples(0)
    for copy in cen_loads[1:] + cof_loads:
        copy.wait()
    lax.fori_loop(0, 16, prepare_centres, 0)

    tn = 512
    pacc[...] = jnp.zeros_like(pacc)

    def data_tile(i, _):
        mine = pl.ds(pl.multiple_of(i // 4 * 512, 512), 512)
        at = pl.ds(pl.multiple_of(i % 4 * tn, tn), tn)
        cross = lax.dot_general(s3[mine, :], c3[at, :], NT, preferred_element_type=f32)
        value = kernel_of(cross + lanes(scol[mine, :], tn // n) + crow[0:1, at])
        hi, lo = halves(value)
        kh[mine, at] = hi
        kl[mine, at] = lo
        w = cof2[at, :]
        pacc[mine, :] += jnp.dot(hi, w, preferred_element_type=f32) + jnp.dot(lo, w, preferred_element_type=f32)
        return 0

    lax.fori_loop(0, 4, data_tile, 0)
    for copy in smp_copies:
        copy.wait_recv()
    prepare_samples(1)
    lax.fori_loop(4, 6, data_tile, 0)
    for pair in FIRST_ROWS:
        await_rows(PLACE[pair])
    relay_rows(0)
    for pair in FIRST_ROWS[::-1]:
        forward_rows(PLACE[pair])
    lax.fori_loop(6, 8, data_tile, 0)
    both = pacc[...].T
    pred[...] = both[0:64] + both[64:128]

    group = [(dx, dz, kk) for dx, dz in PAIRS for kk in (0, 1)][1:]
    p_copies = []
    for s, (dx, dz, kk) in enumerate(group):
        to = centre_of(dx, dz)
        copy = remote(
            pred.at[pl.ds(pl.multiple_of(to * 8, 8), 8), pl.ds(kk * 512, 512)],
            pred_in.at[s], p_send.at[s], p_recv.at[s], (sib if kk else d, to),
        )
        copy.start()
        p_copies.append(copy)
    sends += p_copies

    tgt_load.wait()
    for copy in row_loads:
        copy.wait()

    tm = 512

    def square(j, _):
        for kk in (0, 1):
            v = rows[j, kk]
            hi, lo = halves(v * (-2.0 * SCALE_SQ))
            to = slice(kk * n, kk * n + n)
            r3[to, 0:512] = hi
            r3[to, 512:1024] = hi
            r3[to, 1024:1536] = lo
            rrow[:, to] = norm_of(v).T[0:8, :]
        cols = pl.ds(pl.multiple_of(j * 256, 256), 256)

        def tile(i, _):
            at = pl.ds(pl.multiple_of(i * tm, tm), tm)
            cross = lax.dot_general(c3[at, :], r3[...], NT, preferred_element_type=f32)
            hi, lo = halves(kernel_of(cross + lanes(ccol[at, :], 2) + rrow[0:1, :]))
            th[at, cols] = hi
            tl[at, cols] = lo
            return 0

        lax.fori_loop(0, 2048 // tm, tile, 0)
        return 0

    lax.fori_loop(0, 1, square, 0)

    mine = pl.ds(pl.multiple_of(c * 8, 8), 8)
    for copy in p_copies:
        copy.wait_recv()
    total = pred[mine, 0:512] - tgt[mine, :]
    for s in range(15):
        total += pred_in[s]
    res[0, mine, :] = total
    q_copies = []
    for s, (dx, dz, kk) in enumerate(group):
        copy = remote(
            res.at[0, mine], res.at[kk, mine], q_send.at[s], q_recv.at[s], (sib if kk else d, centre_of(dx, dz))
        )
        copy.start()
        q_copies.append(copy)
    sends += q_copies
    await_relayed(0)
    forward_rows(PLACE[(2, 0)])
    await_forward(1)
    await_forward(2)
    lax.fori_loop(1, 3, square, 0)
    for copy in q_copies:
        copy.wait_recv()
    send_rows(LATER_ROWS)

    for kk in (0, 1):
        hi, lo = halves(res[kk])
        lhs_r[0:64, kk * 512 : kk * 512 + 512] = lo
        lhs_r[64:128, kk * 512 : kk * 512 + 512] = hi
    gy_copies = []
    for dy in (2, 1, 3, 0):
        at = slice(dy * 512, dy * 512 + 512)
        a = jnp.dot(lhs_r[...], kh[:, at], preferred_element_type=f32)
        b = jnp.dot(lhs_r[64:128, :], kl[:, at], preferred_element_type=f32)
        gpart[dy] = a[0:64] + a[64:128] + b
        if dy:
            copy = remote(gpart.at[dy], g_y.at[dy - 1], gy_send.at[dy - 1], gy_recv.at[dy - 1], at_y(dy))
            copy.start()
            gy_copies.append(copy)
    sends += gy_copies
    res_out[...] = res[0]
    await_forward(3)
    await_forward(4)
    lax.fori_loop(3, 5, square, 0)
    for copy in gy_copies:
        copy.wait_recv()
    gsum[...] = gpart[0] + g_y[0] + g_y[1] + g_y[2]
    gz_copies = []
    for dz in (2, 1, 3):
        copy = remote(
            gsum.at[:, pl.ds(dz * n, n)], g_z.at[dz - 1], gz_send.at[dz - 1], gz_recv.at[dz - 1], at_z(dz)
        )
        copy.start()
        gz_copies.append(copy)
    sends += gz_copies
    for pair in LATER_ROWS:
        await_rows(PLACE[pair])
    relay_rows(1)
    for pair in LATER_ROWS:
        forward_rows(PLACE[pair])
    for copy in gz_copies:
        copy.wait_recv()
    gall[0, :, 0:n] = gsum[:, 0:n] + g_z[0] + g_z[1] + g_z[2]

    def spread_z(buf, send, recv):
        copies = []
        for dz in (2, 1, 3):
            to = (4 - dz) % 4
            copy = remote(
                buf.at[0, :, pl.ds(0, n)], buf.at[0, :, pl.ds(to * n, n)], send.at[dz - 1], recv.at[dz - 1], at_z(dz)
            )
            copy.start()
            copies.append(copy)
        sends.extend(copies)
        return copies

    def spread_y(buf, send, recv):
        copies = []
        for dy in (2, 1, 3):
            copy = remote(buf.at[0], buf.at[(4 - dy) % 4], send.at[dy - 1], recv.at[dy - 1], at_y(dy))
            copy.start()
            copies.append(copy)
        sends.extend(copies)
        return copies

    az_copies = spread_z(gall, az_send, az_recv)
    await_forward(5)
    await_forward(6)
    lax.fori_loop(5, 7, square, 0)
    for copy in az_copies:
        copy.wait_recv()
    await_relayed(1)
    forward_rows(7)
    ay_copies = spread_y(gall, ay_send, ay_recv)
    await_forward(7)
    lax.fori_loop(7, 8, square, 0)
    def project(buf, out, arrivals, ones, finish):
        top = 144 if ones else 128
        for dy in (0, 1, 3, 2):
            if dy:
                arrivals[(4 - dy) % 4].wait_recv()
            hi, lo = halves(buf[dy, 0:64, :])
            lhs_u[0:64, :] = lo
            lhs_u[64:128, :] = hi
            k = slice(dy * 512, dy * 512 + 512)

            def part(at):
                a = jnp.dot(lhs_u[0:top, :], th[k, at], preferred_element_type=f32)
                b = jnp.dot(lhs_u[64:top, :], tl[k, at], preferred_element_type=f32)
                total = a[0:64] + a[64:128] + b[0:64]
                out[0:64, at] = total if dy == 0 else out[0:64, at] + total
                if ones:
                    total = a[128:136] + b[64:72]
                    out[64:72, at] = total if dy == 0 else out[64:72, at] + total

            if dy == 2:
                for i in (3, 2, 1, 0):
                    part(slice(i * 512, i * 512 + 512))
                    finish(2 * i + 1)
                    finish(2 * i)
            else:

                def tile(i, _):
                    part(pl.ds(pl.multiple_of(i * 512, 512), 512))
                    return 0

                lax.fori_loop(0, 4, tile, 0)

    def swap_core(part, arrived, send, recv, j):
        copy = remote(part.at[:, pl.ds((2 * j + 1) * n, n)], arrived.at[j], send.at[j], recv.at[j], (sib, c))
        copy.start()
        sends.append(copy)
        return copy

    def to_owner(summed, arrived, send, recv, j):
        copy = remote(summed.at[j], arrived.at[j - 1], send.at[j - 1], recv.at[j - 1], (d, centre_of(*PAIRS[j])))
        copy.start()
        sends.append(copy)
        return copy

    lhs_u[128:144, :] = jnp.ones((16, 512), bf16)
    swaps = {}

    def finish_u(j):
        swaps[j] = swap_core(upart, u_core, uc_send, uc_recv, j)

    project(gall, upart, {i: copy for i, copy in zip((2, 1, 3), ay_copies)}, True, finish_u)
    owners = []
    for j in (7, 6, 5, 4, 3, 2, 1, 0):
        swaps[j].wait_recv()
        usum[j] = upart[:, 2 * j * n : 2 * j * n + n] + u_core[j]
        if j:
            owners.append(to_owner(usum, u_in, ur_send, ur_recv, j))
    for copy in owners:
        copy.wait_recv()
    total = usum[0]
    for s in range(7):
        total += u_in[s]
    uall[0, 0:64, 0:n] = total[0:64]
    uall[0, 64:72, 0:n] = jnp.broadcast_to(jnp.max(total[64:72], axis=1, keepdims=True), (8, n))

    for copy in spread_z(uall, bz_send, bz_recv):
        copy.wait_recv()
    by_copies = spread_y(uall, by_send, by_recv)

    tops = []

    def finish_v(j):
        if not tops:
            largest = uall[0, 64:72, 0:n]
            for dy in range(4):
                for dz in range(4):
                    largest = jnp.maximum(largest, uall[dy, 64:72, dz * n : dz * n + n])
            tops.append(largest)
        vpart[64:72, (2 * j + 1) * n : (2 * j + 2) * n] = tops[0]
        swaps[j] = swap_core(vpart, v_core, vc_send, vc_recv, j)

    project(uall, vpart, {i: copy for i, copy in zip((2, 1, 3), by_copies)}, False, finish_v)
    owners = []
    for j in (7, 6, 5, 4, 3, 2, 1, 0):
        swaps[j].wait_recv()
        vsum[j, 0:64] = vpart[0:64, 2 * j * n : 2 * j * n + n] + v_core[j, 0:64]
        vsum[j, 64:72] = jnp.maximum(tops[0], v_core[j, 64:72])
        if j:
            owners.append(to_owner(vsum, v_in, vr_send, vr_recv, j))
    for copy in owners:
        copy.wait_recv()
    twice = vsum[0, 0:64]
    largest = vsum[0, 64:72]
    for s in range(7):
        twice += v_in[s, 0:64]
        largest = jnp.maximum(largest, v_in[s, 64:72])
    size = jnp.concatenate([1.0 / largest] * 8, axis=0)
    once, grad = uall[0, 0:64, 0:n], gall[0, :, 0:n]
    theta = size * (3.0 * grad - size * (3.0 * once - size * twice))
    new_out[...] = cof[:, 0:n] - LEARNING_RATE * theta

    for copy in sends:
        copy.wait_send()


def hand_over(res_in, new_in, res_out, new_out):
    res_out[...] = res_in[...]
    new_out[...] = new_in[...]


def body(samples, targets, centres, coefficients):
    dma = pltpu.SemaphoreType.DMA
    vmem = pltpu.VMEM
    res_t, new_t = pl.pallas_call(
        step_kernel,
        out_shape=(jax.ShapeDtypeStruct((64, 512), f32), jax.ShapeDtypeStruct((64, 128), f32)),
        in_specs=[pl.BlockSpec(memory_space=pl.ANY)] * 4,
        out_specs=[pl.BlockSpec(memory_space=vmem)] * 2,
        scratch_shapes=[
            vmem((2048, 512), f32), vmem((64, 2048), f32), vmem((2, 512, 512), f32), vmem((64, 512), f32),
            vmem((8, 2, 128, 512), f32),
            vmem((2048, 1536), bf16), vmem((2048, 128), f32), vmem((8, 2048), f32),
            vmem((1024, 1536), bf16), vmem((1024, 128), f32), vmem((256, 1536), bf16), vmem((8, 256), f32),
            vmem((2048, 128), bf16),
            vmem((1024, 2048), bf16), vmem((1024, 2048), bf16), vmem((2048, 2048), bf16), vmem((2048, 2048), bf16),
            vmem((1024, 128), f32), vmem((64, 1024), f32), vmem((15, 8, 512), f32), vmem((2, 64, 512), f32),
            vmem((4, 64, 512), f32), vmem((3, 64, 512), f32), vmem((64, 512), f32), vmem((3, 64, 128), f32),
            vmem((4, 64, 512), f32),
            vmem((72, 2048), f32), vmem((8, 72, 128), f32), vmem((8, 72, 128), f32), vmem((7, 72, 128), f32),
            vmem((4, 72, 512), f32),
            vmem((72, 2048), f32), vmem((8, 72, 128), f32), vmem((8, 72, 128), f32), vmem((7, 72, 128), f32),
            vmem((128, 1024), bf16), vmem((144, 512), bf16),
            dma((37,)), dma((4,)), dma((4,)), dma((8,)), dma((8,)), dma((8,)), dma((8,)), dma((4,)), dma((4,)),
            dma((15,)), dma((15,)), dma((15,)), dma((15,)),
            dma((3,)), dma((3,)), dma((3,)), dma((3,)), dma((3,)), dma((3,)), dma((3,)), dma((3,)),
            dma((8,)), dma((8,)), dma((7,)), dma((7,)), dma((3,)), dma((3,)), dma((3,)), dma((3,)),
            dma((8,)), dma((8,)), dma((7,)), dma((7,)),
        ],
        compiler_params=pltpu.CompilerParams(
            collective_id=0, has_side_effects=True, vmem_limit_bytes=63 * 2**20
        ),
    )(samples, targets.T, centres, coefficients.T)
    res_t, new_t = pl.pallas_call(
        hand_over,
        out_shape=(jax.ShapeDtypeStruct((64, 512), f32), jax.ShapeDtypeStruct((64, 128), f32)),
        in_specs=[pl.BlockSpec(memory_space=vmem)] * 2,
        out_specs=[pl.BlockSpec(memory_space=vmem)] * 2,
    )(res_t, new_t)
    return res_t.T, new_t.T


def solution(mesh):
    return jax.shard_map(
        body,
        mesh=mesh,
        in_specs=(P("dp", None), P("dp", None), P("centre", None), P("centre", None)),
        out_specs=(P("dp", None), P(("centre", "dp"), None)),
        check_vma=False,
    )
```

```python
import functools
import math

import jax
import jax.numpy as jnp
from jax import lax
from jax.experimental import pallas as pl
from jax.experimental.pallas import tpu as pltpu
from jax.sharding import PartitionSpec as P

MESH = pl.DeviceIdType.MESH
f32, bf16 = jnp.float32, jnp.bfloat16
NT = (((1,), (1,)), ((), ()))

SOFTENING = 0.01
KERNEL_SCALE = 0.2
LEARNING_RATE = 4.0
SCALE_SQ = (math.log2(math.e) / KERNEL_SCALE) ** 2
EPS = SOFTENING * SCALE_SQ

PAIRS = ((0, 0), (0, 1), (1, 0), (3, 0), (2, 0), (1, 1), (3, 1), (2, 1))
PLACE = {pair: at for at, pair in enumerate(PAIRS)}
FIRST_ROWS = ((1, 0), (3, 0), (0, 1))
LATER_ROWS = ((1, 1), (3, 1))
SUM_TOP = 40
TOP = 48


def halves(x):
    hi = x.astype(bf16)
    lo = (x - hi.astype(f32)).astype(bf16)
    return hi, lo


def kernel_of(z):
    z = jnp.maximum(z, EPS)
    return jnp.exp2(-(z * lax.rsqrt(z)))


def lanes(x, times):
    return jnp.concatenate([x] * times, axis=1)


def step_kernel(
    samples, targets, centres, coefs, res_out, new_out,
    cen, cof, smp, tgt, rows,
    c3, ccol, crow, s3, scol, r3, rrow, cof2,
    kh, kl, th, tl,
    pacc, pred, pred_in, res,
    gpart, g_y, gsum, g_z, h_z, hsum, h_y, gall,
    upart, u_core, usum, u_in, uall,
    vpart, v_core, vsum, v_in,
    lhs_r, lhs_u,
    loc_sem, smp_send, smp_recv, row_send, row_recv, fwd_send, fwd_recv, rel_send, rel_recv,
    p_send, p_recv, q_send, q_recv,
    gy_send, gy_recv, gz_send, gz_recv, hz_send, hz_recv, hy_send, hy_recv, az_send, az_recv, ay_send, ay_recv,
    uc_send, uc_recv, ur_send, ur_recv, bz_send, bz_recv, by_send, by_recv,
    vc_send, vc_recv, vr_send, vr_recv,
):
    d, c = lax.axis_index("dp"), lax.axis_index("centre")
    core, zh, y = d % 2, (d // 2) % 4, d // 8
    x, zl = c // 2, c % 2
    sib = d + 1 - 2 * core

    def at_y(j):
        return (((y + j) % 4 * 4 + zh) * 2 + core, c)

    def at_z(j):
        return ((y * 4 + (zh + j) % 4) * 2 + core, c)

    def centre_of(dx, dz):
        return (x + dx) % 4 * 2 + (zl + dz) % 2

    def remote(src, dst, send, recv, to):
        return pltpu.make_async_remote_copy(
            src_ref=src, dst_ref=dst, send_sem=send, recv_sem=recv, device_id=to, device_id_type=MESH
        )

    n = 128
    local = []

    def load(src, dst, sem):
        copy = pltpu.make_async_copy(src, dst, sem)
        copy.start()
        local.append(copy)
        return copy

    own_rows = pl.ds(pl.multiple_of(d * n, n), n)
    sib_rows = pl.ds(pl.multiple_of(sib * n, n), n)
    smp_load = load(samples, smp.at[0], loc_sem.at[0])
    cen_loads, cof_loads = [], []
    for b in range(16):
        owner = ((y + b // 4) % 4 * 4 + (zh + b % 4) % 4) * 2 + core
        at = pl.ds(pl.multiple_of(owner * n, n), n)
        cen_loads.append(load(centres.at[at], cen.at[pl.ds(b * n, n)], loc_sem.at[5 + b]))
        cof_loads.append(load(coefs.at[:, at], cof.at[:, pl.ds(b * n, n)], loc_sem.at[21 + b]))
    tgt_load = load(targets, tgt, loc_sem.at[1])
    row_loads = [
        load(centres.at[own_rows], rows.at[0, 0], loc_sem.at[2]),
        load(centres.at[sib_rows], rows.at[0, 1], loc_sem.at[3]),
    ]

    barrier = pltpu.get_barrier_semaphore()
    partners = [(sib, c)] + [at_y(j) for j in (1, 2, 3)] + [at_z(j) for j in (1, 2, 3)]
    for dx, dz in PAIRS[1:]:
        partners += [(d, centre_of(dx, dz)), (sib, centre_of(dx, dz))]
    for to in partners:
        pl.semaphore_signal(barrier, inc=1, device_id=to, device_id_type=MESH)

    sends = []

    def send_rows(pairs):
        for dx, dz in pairs:
            j = PLACE[((4 - dx) % 4, dz)]
            copy = remote(
                cen.at[pl.ds(0, n)], rows.at[j, 0], row_send.at[PLACE[(dx, dz)]], row_recv.at[j], (d, centre_of(dx, dz))
            )
            copy.start()
            sends.append(copy)

    def await_rows(j):
        remote(rows.at[j, 0], rows.at[j, 0], row_send.at[j], row_recv.at[j], (sib, c)).wait_recv()

    def relay_rows(dz):
        far = PLACE[(2, dz)]
        for i, (back, on) in enumerate(((1, 3), (3, 1))):
            part = pl.ds(i * 64, 64)
            copy = remote(
                rows.at[PLACE[(back, dz)], 0, part], rows.at[far, 0, part],
                rel_send.at[dz * 2 + i], rel_recv.at[dz * 2 + i], (d, centre_of(on, 0)),
            )
            copy.start()
            sends.append(copy)

    def await_relayed(dz):
        for i in (0, 1):
            part = rows.at[PLACE[(2, dz)], 0, pl.ds(i * 64, 64)]
            remote(part, part, rel_send.at[dz * 2 + i], rel_recv.at[dz * 2 + i], (sib, c)).wait_recv()

    def forward_rows(j):
        copy = remote(rows.at[j, 0], rows.at[j, 1], fwd_send.at[j], fwd_recv.at[j], (sib, c))
        copy.start()
        sends.append(copy)

    def await_forward(j):
        remote(rows.at[j, 0], rows.at[j, 1], fwd_send.at[j], fwd_recv.at[j], (sib, c)).wait_recv()

    def norms_of(v, down, across):
        hi, lo = halves(v * v * SCALE_SQ)
        out = []
        if down:
            ones = jnp.ones((512, n), bf16)
            out.append(jnp.dot(hi, ones, preferred_element_type=f32) + jnp.dot(lo, ones, preferred_element_type=f32))
        if across:
            ones = jnp.ones((16, 512), bf16)
            a = lax.dot_general(ones, hi, NT, preferred_element_type=f32)
            b = lax.dot_general(ones, lo, NT, preferred_element_type=f32)
            out.append((a + b)[0:8, :])
        return out

    def prepare_samples(half):
        def one(i, _):
            at = pl.ds(pl.multiple_of(i * n, n), n)
            to = pl.ds(pl.multiple_of(half * 512 + i * n, n), n)
            v = smp[half, at, :]
            hi, lo = halves(v * (-2.0 * SCALE_SQ))
            s3[to, 0:512] = hi
            s3[to, 512:1024] = hi
            s3[to, 1024:1536] = lo
            scol[to, :] = norms_of(v, True, False)[0] + EPS
            return 0

        lax.fori_loop(0, 4, one, 0)

    def prepare_centres(i, _):
        at = pl.ds(pl.multiple_of(i * n, n), n)
        v = cen[at, :]
        hi, lo = halves(v)
        c3[at, 0:512] = hi
        c3[at, 512:1024] = lo
        c3[at, 1024:1536] = hi
        down, across = norms_of(v, True, True)
        ccol[at, :] = down + EPS
        crow[:, at] = across
        w = cof[:, at]
        whi = w.astype(bf16).astype(f32)
        cof2[at, :] = jnp.concatenate([whi, w - whi], axis=0).T.astype(bf16)
        return 0

    smp_load.wait()
    prepare_samples(0)
    for group in range(4):
        for b in range(group * 4, group * 4 + 4):
            cen_loads[b].wait()
            cof_loads[b].wait()
        lax.fori_loop(group * 4, group * 4 + 4, prepare_centres, 0)
        if group == 0:
            pl.semaphore_wait(barrier, len(partners))
            smp_copies = []
            for i in range(4):
                at = pl.ds(i * n, n)
                copy = remote(smp.at[0, at], smp.at[1, at], smp_send.at[i], smp_recv.at[i], (sib, c))
                copy.start()
                smp_copies.append(copy)
            sends += smp_copies
            send_rows(FIRST_ROWS)

    tn = 1024
    pacc[...] = jnp.zeros_like(pacc)

    def data_tile(i, _):
        mine = pl.ds(pl.multiple_of(i // 2 * 512, 512), 512)
        at = pl.ds(pl.multiple_of(i % 2 * tn, tn), tn)
        cross = lax.dot_general(s3[mine, :], c3[at, :], NT, preferred_element_type=f32)
        value = kernel_of(cross + lanes(scol[mine, :], tn // n) + crow[0:1, at])
        hi, lo = halves(value)
        kh[mine, at] = hi
        kl[mine, at] = lo
        w = cof2[at, :]
        pacc[mine, :] += jnp.dot(hi, w, preferred_element_type=f32) + jnp.dot(lo, w, preferred_element_type=f32)
        return 0

    lax.fori_loop(0, 2, data_tile, 0)
    for copy in smp_copies:
        copy.wait_recv()
    prepare_samples(1)
    lax.fori_loop(2, 3, data_tile, 0)
    for pair in FIRST_ROWS:
        await_rows(PLACE[pair])
    relay_rows(0)
    for pair in FIRST_ROWS[::-1]:
        forward_rows(PLACE[pair])
    lax.fori_loop(3, 4, data_tile, 0)
    both = pacc[...].T
    pred[...] = both[0:64] + both[64:128]

    group = [(dx, dz, kk) for dx, dz in PAIRS for kk in (0, 1)][1:]
    p_copies = []
    for s, (dx, dz, kk) in enumerate(group):
        to = centre_of(dx, dz)
        copy = remote(
            pred.at[pl.ds(pl.multiple_of(to * 8, 8), 8), pl.ds(kk * 512, 512)],
            pred_in.at[s], p_send.at[s], p_recv.at[s], (sib if kk else d, to),
        )
        copy.start()
        p_copies.append(copy)
    sends += p_copies

    tgt_load.wait()
    for copy in row_loads:
        copy.wait()

    tm = 1024

    def square(j, _):
        for kk in (0, 1):
            v = rows[j, kk]
            hi, lo = halves(v * (-2.0 * SCALE_SQ))
            to = slice(kk * n, kk * n + n)
            r3[to, 0:512] = hi
            r3[to, 512:1024] = hi
            r3[to, 1024:1536] = lo
            rrow[:, to] = norms_of(v, False, True)[0]
        cols = pl.ds(pl.multiple_of(j * 256, 256), 256)

        def tile(i, _):
            at = pl.ds(pl.multiple_of(i * tm, tm), tm)
            cross = lax.dot_general(c3[at, :], r3[...], NT, preferred_element_type=f32)
            hi, lo = halves(kernel_of(cross + lanes(ccol[at, :], 2) + rrow[0:1, :]))
            th[at, cols] = hi
            tl[at, cols] = lo
            return 0

        lax.fori_loop(0, 2048 // tm, tile, 0)
        return 0

    lax.fori_loop(0, 1, square, 0)

    mine = pl.ds(pl.multiple_of(c * 8, 8), 8)
    for copy in p_copies:
        copy.wait_recv()
    total = pred[mine, 0:512] - tgt[mine, :]
    for s in range(15):
        total += pred_in[s]
    res[0, mine, :] = total
    q_copies = []
    for s, (dx, dz, kk) in enumerate(group):
        copy = remote(
            res.at[0, mine], res.at[kk, mine], q_send.at[s], q_recv.at[s], (sib if kk else d, centre_of(dx, dz))
        )
        copy.start()
        q_copies.append(copy)
    sends += q_copies
    await_relayed(0)
    forward_rows(PLACE[(2, 0)])
    await_forward(1)
    await_forward(2)
    lax.fori_loop(1, 3, square, 0)
    for copy in q_copies:
        copy.wait_recv()
    send_rows(LATER_ROWS)

    for kk in (0, 1):
        hi, lo = halves(res[kk])
        lhs_r[0:64, kk * 512 : kk * 512 + 512] = lo
        lhs_r[64:128, kk * 512 : kk * 512 + 512] = hi
    gy_copies = []
    top = pl.ds(0, SUM_TOP)
    low = pl.ds(SUM_TOP, 64 - SUM_TOP)
    for dy in (2, 1, 3, 0):
        at = slice(dy * 512, dy * 512 + 512)
        a = jnp.dot(lhs_r[...], kh[:, at], preferred_element_type=f32)
        b = jnp.dot(lhs_r[64:128, :], kl[:, at], preferred_element_type=f32)
        gpart[dy] = a[0:64] + a[64:128] + b
        if dy:
            copy = remote(gpart.at[dy, top], g_y.at[dy - 1], gy_send.at[dy - 1], gy_recv.at[dy - 1], at_y(dy))
            copy.start()
            gy_copies.append(copy)
    hz_copies = []
    for dz in (2, 1, 3):
        copy = remote(
            gpart.at[:, low, pl.ds(dz * n, n)], h_z.at[dz - 1], hz_send.at[dz - 1], hz_recv.at[dz - 1], at_z(dz)
        )
        copy.start()
        hz_copies.append(copy)
    sends += gy_copies + hz_copies
    res_out[...] = res[0]
    await_forward(3)
    await_forward(4)
    lax.fori_loop(3, 5, square, 0)
    for copy in gy_copies:
        copy.wait_recv()
    gsum[...] = gpart[0, 0:SUM_TOP] + g_y[0] + g_y[1] + g_y[2]
    gz_copies = []
    for dz in (2, 1, 3):
        copy = remote(
            gsum.at[:, pl.ds(dz * n, n)], g_z.at[dz - 1], gz_send.at[dz - 1], gz_recv.at[dz - 1], at_z(dz)
        )
        copy.start()
        gz_copies.append(copy)
    for copy in hz_copies:
        copy.wait_recv()
    hsum[...] = gpart[:, SUM_TOP:64, 0:n] + h_z[0] + h_z[1] + h_z[2]
    hy_copies = []
    for dy in (2, 1, 3):
        copy = remote(hsum.at[dy], h_y.at[dy - 1], hy_send.at[dy - 1], hy_recv.at[dy - 1], at_y(dy))
        copy.start()
        hy_copies.append(copy)
    sends += gz_copies + hy_copies
    for pair in LATER_ROWS:
        await_rows(PLACE[pair])
    relay_rows(1)
    for pair in LATER_ROWS:
        forward_rows(PLACE[pair])
    for copy in gz_copies + hy_copies:
        copy.wait_recv()
    gall[0, 0:SUM_TOP, 0:n] = gsum[:, 0:n] + g_z[0] + g_z[1] + g_z[2]
    gall[0, SUM_TOP:64, 0:n] = hsum[0] + h_y[0] + h_y[1] + h_y[2]

    def spread_first(buf, send, recv):
        rest = buf.shape[1] - TOP
        along_z, along_y = [], []
        for j in (2, 1, 3):
            to = (4 - j) % 4
            copy = remote(
                buf.at[0, pl.ds(0, TOP), pl.ds(0, n)], buf.at[0, pl.ds(0, TOP), pl.ds(to * n, n)],
                send.at[j - 1], recv.at[j - 1], at_z(j),
            )
            copy.start()
            along_z.append(copy)
            part = pl.ds(TOP, rest), pl.ds(0, n)
            copy = remote(buf.at[(0, *part)], buf.at[(to, *part)], send.at[j + 2], recv.at[j + 2], at_y(j))
            copy.start()
            along_y.append(copy)
        sends.extend(along_z + along_y)
        return along_z, along_y

    def spread_rest(buf, send, recv, along_y):
        rest = buf.shape[1] - TOP
        for copy in along_y:
            copy.wait_recv()
        copies = []
        for j in (2, 1, 3):
            to = (4 - j) % 4
            copy = remote(
                buf.at[:, pl.ds(TOP, rest), pl.ds(0, n)], buf.at[:, pl.ds(TOP, rest), pl.ds(to * n, n)],
                send.at[j - 1], recv.at[j - 1], at_z(j),
            )
            copy.start()
            copies.append(copy)
        sends.extend(copies)
        return copies

    def spread_top(buf, send, recv, along_z):
        for copy in along_z:
            copy.wait_recv()
        copies = {}
        for j in (2, 1, 3):
            to = (4 - j) % 4
            part = buf.at[0, pl.ds(0, TOP)]
            copy = remote(part, buf.at[to, pl.ds(0, TOP)], send.at[j + 2], recv.at[j + 2], at_y(j))
            copy.start()
            copies[to] = copy
        sends.extend(copies.values())
        return copies

    along_z, along_y = spread_first(gall, az_send, az_recv)
    await_forward(5)
    lax.fori_loop(5, 6, square, 0)
    rest = spread_rest(gall, ay_send, ay_recv, along_y)
    tops = spread_top(gall, ay_send, ay_recv, along_z)
    await_relayed(1)
    forward_rows(7)
    await_forward(6)
    lax.fori_loop(6, 7, square, 0)
    await_forward(7)
    lax.fori_loop(7, 8, square, 0)
    def project(buf, out, rest, tops, ones, finish):
        top = 144 if ones else 128
        for dy in (0, 1, 3, 2):
            for copy in [tops[dy]] if dy else rest:
                copy.wait_recv()
            hi, lo = halves(buf[dy, 0:64, :])
            lhs_u[0:64, :] = lo
            lhs_u[64:128, :] = hi
            k = slice(dy * 512, dy * 512 + 512)

            def part(at):
                a = jnp.dot(lhs_u[0:top, :], th[k, at], preferred_element_type=f32)
                b = jnp.dot(lhs_u[64:top, :], tl[k, at], preferred_element_type=f32)
                total = a[0:64] + a[64:128] + b[0:64]
                out[0:64, at] = total if dy == 0 else out[0:64, at] + total
                if ones:
                    total = a[128:136] + b[64:72]
                    out[64:72, at] = total if dy == 0 else out[64:72, at] + total

            if dy == 2:
                for i in (3, 2, 1, 0):
                    part(slice(i * 512, i * 512 + 512))
                    finish(2 * i + 1)
                    finish(2 * i)
            else:

                def tile(i, _):
                    part(pl.ds(pl.multiple_of(i * 512, 512), 512))
                    return 0

                lax.fori_loop(0, 4, tile, 0)

    def swap_core(part, arrived, send, recv, j):
        copy = remote(part.at[:, pl.ds((2 * j + 1) * n, n)], arrived.at[j], send.at[j], recv.at[j], (sib, c))
        copy.start()
        sends.append(copy)
        return copy

    def to_owner(summed, arrived, send, recv, j):
        copy = remote(summed.at[j], arrived.at[j - 1], send.at[j - 1], recv.at[j - 1], (d, centre_of(*PAIRS[j])))
        copy.start()
        sends.append(copy)
        return copy

    lhs_u[128:144, :] = jnp.ones((16, 512), bf16)
    swaps = {}

    def finish_u(j):
        swaps[j] = swap_core(upart, u_core, uc_send, uc_recv, j)

    project(gall, upart, rest, tops, True, finish_u)
    owners = []
    for j in (7, 6, 5, 4, 3, 2, 1, 0):
        swaps[j].wait_recv()
        usum[j] = upart[:, 2 * j * n : 2 * j * n + n] + u_core[j]
        if j:
            owners.append(to_owner(usum, u_in, ur_send, ur_recv, j))
    for copy in owners:
        copy.wait_recv()
    total = usum[0]
    for s in range(7):
        total += u_in[s]
    uall[0, 0:64, 0:n] = total[0:64]
    uall[0, 64:72, 0:n] = jnp.broadcast_to(jnp.max(total[64:72], axis=1, keepdims=True), (8, n))

    along_z, along_y = spread_first(uall, bz_send, bz_recv)
    rest = spread_rest(uall, by_send, by_recv, along_y)
    tops = spread_top(uall, by_send, by_recv, along_z)

    found = []

    def finish_v(j):
        if not found:
            largest = uall[0, 64:72, 0:n]
            for dy in range(4):
                for dz in range(4):
                    largest = jnp.maximum(largest, uall[dy, 64:72, dz * n : dz * n + n])
            found.append(largest)
        vpart[64:72, (2 * j + 1) * n : (2 * j + 2) * n] = found[0]
        swaps[j] = swap_core(vpart, v_core, vc_send, vc_recv, j)

    project(uall, vpart, rest, tops, False, finish_v)
    owners = []
    for j in (7, 6, 5, 4, 3, 2, 1, 0):
        swaps[j].wait_recv()
        vsum[j, 0:64] = vpart[0:64, 2 * j * n : 2 * j * n + n] + v_core[j, 0:64]
        vsum[j, 64:72] = jnp.maximum(found[0], v_core[j, 64:72])
        if j:
            owners.append(to_owner(vsum, v_in, vr_send, vr_recv, j))
    for copy in owners:
        copy.wait_recv()
    twice = vsum[0, 0:64]
    largest = vsum[0, 64:72]
    for s in range(7):
        twice += v_in[s, 0:64]
        largest = jnp.maximum(largest, v_in[s, 64:72])
    size = jnp.concatenate([1.0 / largest] * 8, axis=0)
    once, grad = uall[0, 0:64, 0:n], gall[0, :, 0:n]
    theta = size * (3.0 * grad - size * (3.0 * once - size * twice))
    new_out[...] = cof[:, 0:n] - LEARNING_RATE * theta

    for copy in sends:
        copy.wait_send()


def hand_over(res_in, new_in, res_out, new_out):
    res_out[...] = res_in[...]
    new_out[...] = new_in[...]


def body(samples, targets, centres, coefficients):
    dma = pltpu.SemaphoreType.DMA
    vmem = pltpu.VMEM
    res_t, new_t = pl.pallas_call(
        step_kernel,
        out_shape=(jax.ShapeDtypeStruct((64, 512), f32), jax.ShapeDtypeStruct((64, 128), f32)),
        in_specs=[pl.BlockSpec(memory_space=pl.ANY)] * 4,
        out_specs=[pl.BlockSpec(memory_space=vmem)] * 2,
        scratch_shapes=[
            vmem((2048, 512), f32), vmem((64, 2048), f32), vmem((2, 512, 512), f32), vmem((64, 512), f32),
            vmem((8, 2, 128, 512), f32),
            vmem((2048, 1536), bf16), vmem((2048, 128), f32), vmem((8, 2048), f32),
            vmem((1024, 1536), bf16), vmem((1024, 128), f32), vmem((256, 1536), bf16), vmem((8, 256), f32),
            vmem((2048, 128), bf16),
            vmem((1024, 2048), bf16), vmem((1024, 2048), bf16), vmem((2048, 2048), bf16), vmem((2048, 2048), bf16),
            vmem((1024, 128), f32), vmem((64, 1024), f32), vmem((15, 8, 512), f32), vmem((2, 64, 512), f32),
            vmem((4, 64, 512), f32), vmem((3, SUM_TOP, 512), f32), vmem((SUM_TOP, 512), f32), vmem((3, SUM_TOP, 128), f32),
            vmem((3, 4, 64 - SUM_TOP, 128), f32), vmem((4, 64 - SUM_TOP, 128), f32), vmem((3, 64 - SUM_TOP, 128), f32),
            vmem((4, 64, 512), f32),
            vmem((72, 2048), f32), vmem((8, 72, 128), f32), vmem((8, 72, 128), f32), vmem((7, 72, 128), f32),
            vmem((4, 72, 512), f32),
            vmem((72, 2048), f32), vmem((8, 72, 128), f32), vmem((8, 72, 128), f32), vmem((7, 72, 128), f32),
            vmem((128, 1024), bf16), vmem((144, 512), bf16),
            dma((37,)), dma((4,)), dma((4,)), dma((8,)), dma((8,)), dma((8,)), dma((8,)), dma((4,)), dma((4,)),
            dma((15,)), dma((15,)), dma((15,)), dma((15,)),
            dma((3,)), dma((3,)), dma((3,)), dma((3,)), dma((3,)), dma((3,)), dma((3,)), dma((3,)),
            dma((6,)), dma((6,)), dma((6,)), dma((6,)),
            dma((8,)), dma((8,)), dma((7,)), dma((7,)), dma((6,)), dma((6,)), dma((6,)), dma((6,)),
            dma((8,)), dma((8,)), dma((7,)), dma((7,)),
        ],
        compiler_params=pltpu.CompilerParams(
            collective_id=0, has_side_effects=True, vmem_limit_bytes=63 * 2**20
        ),
    )(samples, targets.T, centres, coefficients.T)
    res_t, new_t = pl.pallas_call(
        hand_over,
        out_shape=(jax.ShapeDtypeStruct((64, 512), f32), jax.ShapeDtypeStruct((64, 128), f32)),
        in_specs=[pl.BlockSpec(memory_space=vmem)] * 2,
        out_specs=[pl.BlockSpec(memory_space=vmem)] * 2,
    )(res_t, new_t)
    return res_t.T, new_t.T


def solution(mesh):
    return jax.shard_map(
        body,
        mesh=mesh,
        in_specs=(P("dp", None), P("dp", None), P("centre", None), P("centre", None)),
        out_specs=(P("dp", None), P(("centre", "dp"), None)),
        check_vma=False,
    )
```

```python
import functools
import math

import jax
import jax.numpy as jnp
from jax import lax
from jax.experimental import pallas as pl
from jax.experimental.pallas import tpu as pltpu
from jax.sharding import PartitionSpec as P

MESH = pl.DeviceIdType.MESH
f32, bf16 = jnp.float32, jnp.bfloat16
NT = (((1,), (1,)), ((), ()))

SOFTENING = 0.01
KERNEL_SCALE = 0.2
LEARNING_RATE = 4.0
SCALE_SQ = (math.log2(math.e) / KERNEL_SCALE) ** 2
EPS = SOFTENING * SCALE_SQ

PAIRS = ((0, 0), (1, 0), (3, 0), (2, 0), (0, 1), (1, 1), (3, 1), (2, 1))
PLACE = {pair: at for at, pair in enumerate(PAIRS)}
FIRST_ROWS = ((1, 0), (3, 0), (0, 1))
LATER_ROWS = ((1, 1), (3, 1))
SUM_TOP = 40
TOP = 48


def halves(x):
    hi = x.astype(bf16)
    lo = (x - hi.astype(f32)).astype(bf16)
    return hi, lo


def kernel_of(z):
    z = jnp.maximum(z, EPS)
    return jnp.exp2(-(z * lax.rsqrt(z)))


def lanes(x, times):
    return jnp.concatenate([x] * times, axis=1)


def near_first(t):
    return t + t // 2 - 2 * (t // 3)


def loop(start, stop, f):
    def step(i, _):
        f(i)
        return 0

    lax.fori_loop(start, stop, step, 0)


def step_kernel(
    samples, targets, centres, coefs, res_out, new_out,
    cen, cof, smp, tgt, rows,
    c3, ccol, crow, s3, scol, r3, rrow, cof2,
    kh, kl, th, tl,
    pacc, pred, pred_in, res,
    gpart, g_y, gsum, g_z, h_z, hsum, h_y,
    whole, part, other, summed, arrived, lhs_r, lhs_u,
    loc_sem, smp_send, smp_recv, row_send, row_recv, fwd_send, fwd_recv, rel_send, rel_recv,
    p_send, p_recv, q_send, q_recv,
    gy_send, gy_recv, gz_send, gz_recv, hz_send, hz_recv, hy_send, hy_recv,
    a_send, a_recv, b_send, b_recv, c_send, c_recv, o_send, o_recv,
):
    n = 128
    d, c = lax.axis_index("dp"), lax.axis_index("centre")
    core, zh, y = d % 2, (d // 2) % 4, d // 8
    x, zl = c // 2, c % 2
    sib = d + 1 - 2 * core
    mine = pl.ds(pl.multiple_of(c * 8, 8), 8)
    own_rows = pl.ds(pl.multiple_of(d * n, n), n)
    sib_rows = pl.ds(pl.multiple_of(sib * n, n), n)

    def at_y(j):
        return (((y + j) % 4 * 4 + zh) * 2 + core, c)

    def at_z(j):
        return ((y * 4 + (zh + j) % 4) * 2 + core, c)

    def centre_of(dx, dz):
        return (x + dx) % 4 * 2 + (zl + dz) % 2

    def remote(src, dst, send, recv, to):
        return pltpu.make_async_remote_copy(
            src_ref=src, dst_ref=dst, send_sem=send, recv_sem=recv, device_id=to, device_id_type=MESH
        )

    def got(like, sem):
        remote(like, like, sem, sem, (sib, c)).wait_recv()

    def sent(like, sem):
        remote(like, like, sem, sem, (sib, c)).wait_send()

    def block_loads(b):
        owner = ((y + b // 4) % 4 * 4 + (zh + b % 4) % 4) * 2 + core
        at = pl.ds(pl.multiple_of(owner * n, n), n)
        to = pl.ds(pl.multiple_of(b * n, n), n)
        return (
            pltpu.make_async_copy(centres.at[at], cen.at[to], loc_sem.at[4 + b]),
            pltpu.make_async_copy(coefs.at[:, at], cof.at[:, to], loc_sem.at[20 + b]),
        )

    smp_load = pltpu.make_async_copy(samples, smp.at[0], loc_sem.at[0])
    late_loads = (
        pltpu.make_async_copy(targets, tgt, loc_sem.at[1]),
        pltpu.make_async_copy(centres.at[own_rows], rows.at[0, 0], loc_sem.at[2]),
        pltpu.make_async_copy(centres.at[sib_rows], rows.at[0, 1], loc_sem.at[3]),
    )
    smp_load.start()

    @functools.partial(loop, 0, 16)
    def _(b):
        for copy in block_loads(b):
            copy.start()

    for copy in late_loads:
        copy.start()

    barrier = pltpu.get_barrier_semaphore()
    partners = [(sib, c)] + [at_y(j) for j in (1, 2, 3)] + [at_z(j) for j in (1, 2, 3)]
    for dx, dz in PAIRS[1:]:
        partners += [(d, centre_of(dx, dz)), (sib, centre_of(dx, dz))]
    for to in partners:
        pl.semaphore_signal(barrier, inc=1, device_id=to, device_id_type=MESH)

    def send_rows(pairs):
        for dx, dz in pairs:
            j = PLACE[((4 - dx) % 4, dz)]
            remote(
                cen.at[pl.ds(0, n)], rows.at[j, 0], row_send.at[PLACE[(dx, dz)]], row_recv.at[j], (d, centre_of(dx, dz))
            ).start()

    def relay_rows(dz):
        far = PLACE[(2, dz)]
        for i, (back, on) in enumerate(((1, 3), (3, 1))):
            half = pl.ds(i * 64, 64)
            remote(
                rows.at[PLACE[(back, dz)], 0, half], rows.at[far, 0, half],
                rel_send.at[dz * 2 + i], rel_recv.at[dz * 2 + i], (d, centre_of(on, 0)),
            ).start()

    def await_relayed(dz):
        for i in (0, 1):
            got(rows.at[PLACE[(2, dz)], 0, pl.ds(i * 64, 64)], rel_recv.at[dz * 2 + i])

    def forward_rows(j):
        remote(rows.at[j, 0], rows.at[j, 1], fwd_send.at[j], fwd_recv.at[j], (sib, c)).start()

    def pass_on(pairs, dz):
        for pair in pairs:
            got(rows.at[PLACE[pair], 0], row_recv.at[PLACE[pair]])
        relay_rows(dz)
        for pair in pairs:
            forward_rows(PLACE[pair])

    def norm_of(v):
        total = jnp.sum(v * v, axis=1, keepdims=True) * SCALE_SQ
        return jnp.broadcast_to(total, (n, n))

    def prepare_samples(half):
        @functools.partial(loop, 0, 4)
        def _(i):
            at = pl.ds(pl.multiple_of(i * n, n), n)
            to = pl.ds(pl.multiple_of(half * 512 + i * n, n), n)
            v = smp[half, at, :]
            hi, lo = halves(v * (-2.0 * SCALE_SQ))
            s3[to, 0:512] = hi
            s3[to, 512:1024] = hi
            s3[to, 1024:1536] = lo
            scol[to, :] = norm_of(v) + EPS

    smp_load.wait()
    prepare_samples(0)

    @functools.partial(loop, 0, 16)
    def _(b):
        for copy in block_loads(b):
            copy.wait()
        at = pl.ds(pl.multiple_of(b * n, n), n)
        v = cen[at, :]
        hi, lo = halves(v)
        c3[at, 0:512] = hi
        c3[at, 512:1024] = lo
        c3[at, 1024:1536] = hi
        norms = norm_of(v)
        ccol[at, :] = norms + EPS
        crow[:, at] = norms.T[0:8, :]
        w = cof[:, at]
        whi = w.astype(bf16).astype(f32)
        cof2[at, :] = jnp.concatenate([whi, w - whi], axis=0).T.astype(bf16)

        @pl.when(b == 5)
        def _():
            pl.semaphore_wait(barrier, len(partners))
            for i in range(4):
                at = pl.ds(i * n, n)
                remote(smp.at[0, at], smp.at[1, at], smp_send.at[i], smp_recv.at[i], (sib, c)).start()
            send_rows(FIRST_ROWS)

    tn = 512
    pacc[...] = jnp.zeros_like(pacc)

    @functools.partial(loop, 0, 8)
    def _(i):
        @pl.when(i == 4)
        def _():
            for k in range(4):
                got(smp.at[1, pl.ds(k * n, n)], smp_recv.at[k])
            prepare_samples(1)

        @pl.when(i == 6)
        def _():
            pass_on(FIRST_ROWS, 0)

        these = pl.ds(pl.multiple_of(i // 4 * 512, 512), 512)
        at = pl.ds(pl.multiple_of(i % 4 * tn, tn), tn)
        cross = lax.dot_general(s3[these, :], c3[at, :], NT, preferred_element_type=f32)
        value = kernel_of(cross + lanes(scol[these, :], tn // n) + crow[0:1, at])
        hi, lo = halves(value)
        kh[these, at] = hi
        kl[these, at] = lo
        w = cof2[at, :]
        pacc[these, :] += jnp.dot(hi, w, preferred_element_type=f32) + jnp.dot(lo, w, preferred_element_type=f32)

    both = pacc[...].T
    pred[...] = both[0:64] + both[64:128]

    def member(s):
        dx, dz, kk = s // 4, s // 2 % 2, s % 2
        return centre_of(dx, dz), d + kk * (sib - d), kk

    @functools.partial(loop, 1, 16)
    def _(s):
        to, at_d, kk = member(s)
        remote(
            pred.at[pl.ds(pl.multiple_of(to * 8, 8), 8), pl.ds(pl.multiple_of(kk * 512, 512), 512)],
            pred_in.at[s - 1], p_send.at[s - 1], p_recv.at[s - 1], (at_d, to),
        ).start()

    for copy in late_loads:
        copy.wait()

    def residuals():
        loop(0, 15, lambda s: got(pred_in.at[s], p_recv.at[s]))
        total = pred[mine, 0:512] - tgt[mine, :]
        for s in range(15):
            total += pred_in[s]
        res[0, mine, :] = total

        @functools.partial(loop, 1, 16)
        def _(s):
            to, at_d, kk = member(s)
            remote(res.at[0, mine], res.at[kk, mine], q_send.at[s - 1], q_recv.at[s - 1], (at_d, to)).start()

        await_relayed(0)
        forward_rows(PLACE[(2, 0)])
        got(rows.at[1, 0], fwd_recv.at[1])
        got(rows.at[2, 0], fwd_recv.at[2])

    top, low = pl.ds(0, SUM_TOP), pl.ds(SUM_TOP, 64 - SUM_TOP)

    def gradients():
        loop(0, 15, lambda s: got(res.at[0, pl.ds(0, 8)], q_recv.at[s]))
        send_rows(LATER_ROWS)
        for kk in (0, 1):
            hi, lo = halves(res[kk])
            lhs_r[0:64, kk * 512 : kk * 512 + 512] = lo
            lhs_r[64:128, kk * 512 : kk * 512 + 512] = hi

        @functools.partial(loop, 0, 4)
        def _(t):
            dy = (t + 1) % 4
            at = pl.ds(pl.multiple_of(dy * 512, 512), 512)
            a = jnp.dot(lhs_r[...], kh[:, at], preferred_element_type=f32)
            b = jnp.dot(lhs_r[64:128, :], kl[:, at], preferred_element_type=f32)
            gpart[dy] = a[0:64] + a[64:128] + b

            @pl.when(t < 3)
            def _():
                remote(gpart.at[dy, top], g_y.at[t], gy_send.at[t], gy_recv.at[t], at_y(t + 1)).start()

        for j in (1, 2, 3):
            remote(
                gpart.at[:, low, pl.ds(j * n, n)], h_z.at[j - 1], hz_send.at[j - 1], hz_recv.at[j - 1], at_z(j)
            ).start()
        res_out[...] = res[0]
        got(rows.at[3, 0], fwd_recv.at[3])
        got(rows.at[4, 0], fwd_recv.at[4])

    first, rest = pl.ds(0, TOP), pl.ds(TOP, 72 - TOP)
    start = pl.ds(0, n)

    def spread_first(it):
        for j in (1, 2, 3):
            to = 4 - j
            remote(
                whole.at[it, 0, first, start], whole.at[it, 0, first, pl.ds(to * n, n)],
                a_send.at[it, j - 1], a_recv.at[it, j - 1], at_z(j),
            ).start()
            remote(
                whole.at[it, 0, rest, start], whole.at[it, to, rest, start],
                a_send.at[it, j + 2], a_recv.at[it, j + 2], at_y(j),
            ).start()

    def spread_more(it):
        for j in (1, 2, 3):
            got(whole.at[it, 0, rest, start], a_recv.at[it, j + 2])
        for j in (1, 2, 3):
            to = 4 - j
            remote(
                whole.at[it, :, rest, start], whole.at[it, :, rest, pl.ds(to * n, n)],
                b_send.at[it, j - 1], b_recv.at[it, j - 1], at_z(j),
            ).start()
        for j in (1, 2, 3):
            got(whole.at[it, 0, first, start], a_recv.at[it, j - 1])
        for j in (1, 2, 3):
            remote(
                whole.at[it, 0, first], whole.at[it, 4 - j, first],
                b_send.at[it, j + 2], b_recv.at[it, j + 2], at_y(j),
            ).start()

    def sum_gradients():
        for j in range(3):
            got(g_y.at[j], gy_recv.at[j])
        gsum[...] = gpart[0, 0:SUM_TOP] + g_y[0] + g_y[1] + g_y[2]
        for j in (1, 2, 3):
            remote(
                gsum.at[:, pl.ds(j * n, n)], g_z.at[j - 1], gz_send.at[j - 1], gz_recv.at[j - 1], at_z(j)
            ).start()
        for j in range(3):
            got(h_z.at[j], hz_recv.at[j])
        hsum[...] = gpart[:, SUM_TOP:64, 0:n] + h_z[0] + h_z[1] + h_z[2]
        for j in (1, 2, 3):
            remote(hsum.at[j], h_y.at[j - 1], hy_send.at[j - 1], hy_recv.at[j - 1], at_y(j)).start()
        pass_on(LATER_ROWS, 1)
        for j in range(3):
            got(g_z.at[j], gz_recv.at[j])
            got(h_y.at[j], hy_recv.at[j])
        whole[0, 0, 0:SUM_TOP, 0:n] = gsum[:, 0:n] + g_z[0] + g_z[1] + g_z[2]
        whole[0, 0, SUM_TOP:64, 0:n] = hsum[0] + h_y[0] + h_y[1] + h_y[2]
        whole[0, 0, 64:72, 0:n] = jnp.zeros((8, n), f32)
        spread_first(0)
        got(rows.at[5, 0], fwd_recv.at[5])

    def spread_gradients():
        spread_more(0)
        await_relayed(1)
        forward_rows(7)
        got(rows.at[6, 0], fwd_recv.at[6])

    tm = 1024

    @functools.partial(loop, 0, 8)
    def _(j):
        for kk in (0, 1):
            v = rows[j, kk]
            hi, lo = halves(v * (-2.0 * SCALE_SQ))
            to = slice(kk * n, kk * n + n)
            r3[to, 0:512] = hi
            r3[to, 512:1024] = hi
            r3[to, 1024:1536] = lo
            rrow[:, to] = norm_of(v).T[0:8, :]
        cols = pl.ds(pl.multiple_of(j * 256, 256), 256)

        @functools.partial(loop, 0, 2048 // tm)
        def _(i):
            at = pl.ds(pl.multiple_of(i * tm, tm), tm)
            cross = lax.dot_general(c3[at, :], r3[...], NT, preferred_element_type=f32)
            hi, lo = halves(kernel_of(cross + lanes(ccol[at, :], 2) + rrow[0:1, :]))
            th[at, cols] = hi
            tl[at, cols] = lo

        pl.when(j == 0)(residuals)
        pl.when(j == 2)(gradients)
        pl.when(j == 4)(sum_gradients)
        pl.when(j == 5)(spread_gradients)

        @pl.when(j == 6)
        def _():
            got(rows.at[7, 0], fwd_recv.at[7])

    lhs_u[128:144, :] = jnp.ones((16, 512), bf16)
    part[...] = jnp.zeros_like(part)

    @functools.partial(loop, 0, 2)
    def _(it):
        @functools.partial(loop, 0, 4)
        def _(t):
            dy = near_first(t)

            @pl.when(t == 0)
            def _():
                for j in range(3):
                    got(whole.at[0, :, rest, start], b_recv.at[it, j])

            @pl.when(t > 0)
            def _():
                got(whole.at[0, 0, first], b_recv.at[it, 6 - dy])

            hi, lo = halves(whole[it, dy, 0:64, :])
            lhs_u[0:64, :] = lo
            lhs_u[64:128, :] = hi
            k = pl.ds(pl.multiple_of(dy * 512, 512), 512)

            @functools.partial(loop, 0, 4)
            def _(back):
                i = 3 - back
                at = pl.ds(pl.multiple_of(i * 512, 512), 512)
                a = jnp.dot(lhs_u[...], th[k, at], preferred_element_type=f32)
                b = jnp.dot(lhs_u[64:144, :], tl[k, at], preferred_element_type=f32)
                part[it, 0:64, at] += a[0:64] + a[64:128] + b[0:64]
                part[it, 64:72, at] += a[128:136] + b[64:72]

                @pl.when(t == 3)
                def _():
                    @pl.when(it == 1)
                    def _():
                        largest = whole[1, 0, 64:72, 0:n]
                        for e in range(1, 16):
                            largest = jnp.maximum(largest, whole[1, e // 4, 64:72, e % 4 * n : e % 4 * n + n])
                        largest = lanes(largest, 4)
                        part[1, 64:72, at] = largest

                    for j in (2 * i + 1, 2 * i):
                        theirs = pl.ds(pl.multiple_of((2 * j + 1) * n, n), n)
                        remote(
                            part.at[it, :, theirs], other.at[it, j], c_send.at[it, j], c_recv.at[it, j], (sib, c)
                        ).start()

        def added(a, b):
            return jnp.concatenate([a[0:64] + b[0:64], jnp.where(it == 1, jnp.maximum(a[64:72], b[64:72]), a[64:72] + b[64:72])])

        @functools.partial(loop, 0, 8)
        def _(back):
            j = 7 - back
            got(other.at[0, 0], c_recv.at[it, j])
            ours = pl.ds(pl.multiple_of(2 * j * n, n), n)
            summed[it, j] = added(part[it, :, ours], other[it, j])

            @pl.when(j > 0)
            def _():
                to = centre_of(near_first(j % 4), j // 4)
                remote(
                    summed.at[it, j], arrived.at[it, j - 1], o_send.at[it, j - 1], o_recv.at[it, j - 1], (d, to)
                ).start()

        loop(0, 7, lambda s: got(arrived.at[0, 0], o_recv.at[it, s]))
        total = summed[it, 0]
        for s in range(7):
            total = added(total, arrived[it, s])

        @pl.when(it == 0)
        def _():
            whole[1, 0, 0:64, 0:n] = total[0:64]
            whole[1, 0, 64:72, 0:n] = jnp.broadcast_to(jnp.max(total[64:72], axis=1, keepdims=True), (8, n))
            spread_first(1)
            spread_more(1)

        @pl.when(it == 1)
        def _():
            size = jnp.concatenate([1.0 / total[64:72]] * 8, axis=0)
            once, grad = whole[1, 0, 0:64, 0:n], whole[0, 0, 0:64, 0:n]
            theta = size * (3.0 * grad - size * (3.0 * once - size * total[0:64]))
            new_out[...] = cof[:, 0:n] - LEARNING_RATE * theta

    for i in range(4):
        sent(smp.at[0, pl.ds(0, n)], smp_send.at[i])
        sent(rows.at[0, 0, pl.ds(0, 64)], rel_send.at[i])
    for pair in FIRST_ROWS + LATER_ROWS:
        sent(rows.at[0, 0], row_send.at[PLACE[pair]])
    loop(1, 8, lambda j: sent(rows.at[0, 0], fwd_send.at[j]))

    @functools.partial(loop, 0, 15)
    def _(s):
        sent(pred_in.at[0], p_send.at[s])
        sent(pred_in.at[0], q_send.at[s])

    @functools.partial(loop, 0, 3)
    def _(j):
        sent(g_y.at[0], gy_send.at[j])
        sent(g_z.at[0], gz_send.at[j])
        sent(h_z.at[0], hz_send.at[j])
        sent(h_y.at[0], hy_send.at[j])
        for it in (0, 1):
            sent(whole.at[0, 0, first, start], a_send.at[it, j])
            sent(whole.at[0, 0, rest, start], a_send.at[it, j + 3])
            sent(whole.at[0, :, rest, start], b_send.at[it, j])
            sent(whole.at[0, 0, first], b_send.at[it, j + 3])

    @functools.partial(loop, 0, 8)
    def _(j):
        for it in (0, 1):
            sent(other.at[0, 0], c_send.at[it, j])

            @pl.when(j > 0)
            def _():
                sent(other.at[0, 0], o_send.at[it, j - 1])


def hand_over(res_in, new_in, res_out, new_out):
    res_out[...] = res_in[...]
    new_out[...] = new_in[...]


def body(samples, targets, centres, coefficients):
    dma = pltpu.SemaphoreType.DMA
    vmem = pltpu.VMEM
    res_t, new_t = pl.pallas_call(
        step_kernel,
        out_shape=(jax.ShapeDtypeStruct((64, 512), f32), jax.ShapeDtypeStruct((64, 128), f32)),
        in_specs=[pl.BlockSpec(memory_space=pl.ANY)] * 4,
        out_specs=[pl.BlockSpec(memory_space=vmem)] * 2,
        scratch_shapes=[
            vmem((2048, 512), f32), vmem((64, 2048), f32), vmem((2, 512, 512), f32), vmem((64, 512), f32),
            vmem((8, 2, 128, 512), f32),
            vmem((2048, 1536), bf16), vmem((2048, 128), f32), vmem((8, 2048), f32),
            vmem((1024, 1536), bf16), vmem((1024, 128), f32), vmem((256, 1536), bf16), vmem((8, 256), f32),
            vmem((2048, 128), bf16),
            vmem((1024, 2048), bf16), vmem((1024, 2048), bf16), vmem((2048, 2048), bf16), vmem((2048, 2048), bf16),
            vmem((1024, 128), f32), vmem((64, 1024), f32), vmem((15, 8, 512), f32), vmem((2, 64, 512), f32),
            vmem((4, 64, 512), f32), vmem((3, SUM_TOP, 512), f32), vmem((SUM_TOP, 512), f32), vmem((3, SUM_TOP, 128), f32),
            vmem((3, 4, 64 - SUM_TOP, 128), f32), vmem((4, 64 - SUM_TOP, 128), f32), vmem((3, 64 - SUM_TOP, 128), f32),
            vmem((2, 4, 72, 512), f32), vmem((2, 72, 2048), f32), vmem((2, 8, 72, 128), f32), vmem((2, 8, 72, 128), f32),
            vmem((2, 7, 72, 128), f32), vmem((128, 1024), bf16), vmem((144, 512), bf16),
            dma((36,)), dma((4,)), dma((4,)), dma((8,)), dma((8,)), dma((8,)), dma((8,)), dma((4,)), dma((4,)),
            dma((15,)), dma((15,)), dma((15,)), dma((15,)),
            dma((3,)), dma((3,)), dma((3,)), dma((3,)), dma((3,)), dma((3,)), dma((3,)), dma((3,)),
            dma((2, 6)), dma((2, 6)), dma((2, 6)), dma((2, 6)),
            dma((2, 8)), dma((2, 8)), dma((2, 7)), dma((2, 7)),
        ],
        compiler_params=pltpu.CompilerParams(
            collective_id=0, has_side_effects=True, vmem_limit_bytes=63 * 2**20
        ),
    )(samples, targets.T, centres, coefficients.T)
    res_t, new_t = pl.pallas_call(
        hand_over,
        out_shape=(jax.ShapeDtypeStruct((64, 512), f32), jax.ShapeDtypeStruct((64, 128), f32)),
        in_specs=[pl.BlockSpec(memory_space=vmem)] * 2,
        out_specs=[pl.BlockSpec(memory_space=vmem)] * 2,
    )(res_t, new_t)
    return res_t.T, new_t.T


def solution(mesh):
    return jax.shard_map(
        body,
        mesh=mesh,
        in_specs=(P("dp", None), P("dp", None), P("centre", None), P("centre", None)),
        out_specs=(P("dp", None), P(("centre", "dp"), None)),
        check_vma=False,
    )
```

```python
import functools
import math

import jax
import jax.numpy as jnp
from jax import lax
from jax.experimental import pallas as pl
from jax.experimental.pallas import tpu as pltpu
from jax.sharding import PartitionSpec as P

MESH = pl.DeviceIdType.MESH
f32, bf16 = jnp.float32, jnp.bfloat16
NT = (((1,), (1,)), ((), ()))

SOFTENING = 0.01
KERNEL_SCALE = 0.2
LEARNING_RATE = 4.0
SCALE_SQ = (math.log2(math.e) / KERNEL_SCALE) ** 2
EPS = SOFTENING * SCALE_SQ

PAIRS = ((0, 0), (1, 0), (3, 0), (2, 0), (0, 1), (1, 1), (3, 1), (2, 1))
PLACE = {pair: at for at, pair in enumerate(PAIRS)}
FIRST_ROWS = ((1, 0), (3, 0), (0, 1))
LATER_ROWS = ((1, 1), (3, 1))
SUM_TOP = 40
TOP = 48


def halves(x):
    hi = x.astype(bf16)
    lo = (x - hi.astype(f32)).astype(bf16)
    return hi, lo


def kernel_of(z):
    z = jnp.maximum(z, EPS)
    return jnp.exp2(-(z * lax.rsqrt(z)))


def lanes(x, times):
    return jnp.concatenate([x] * times, axis=1)


def near_first(t):
    return t + t // 2 - 2 * (t // 3)


def loop(start, stop, f):
    def step(i, _):
        f(i)
        return 0

    lax.fori_loop(start, stop, step, 0)


def step_kernel(
    samples, targets, centres, coefs, res_out, new_out,
    cen, cof, smp, tgt, rows,
    c3, ccol, crow, s3, scol, r3, rrow, cof2,
    kh, kl, th, tl,
    pacc, pred, pred_in, res,
    gpart, g_y, gsum, g_z, h_z, hsum, h_y,
    whole, part, other, summed, arrived, lhs_r, lhs_u,
    loc_sem, smp_send, smp_recv, row_send, row_recv, fwd_send, fwd_recv, rel_send, rel_recv,
    p_send, p_recv, q_send, q_recv,
    gy_send, gy_recv, gz_send, gz_recv, hz_send, hz_recv, hy_send, hy_recv,
    a_send, a_recv, b_send, b_recv, c_send, c_recv, o_send, o_recv,
):
    n = 128
    d, c = lax.axis_index("dp"), lax.axis_index("centre")
    core, zh, y = d % 2, (d // 2) % 4, d // 8
    x, zl = c // 2, c % 2
    sib = d + 1 - 2 * core
    mine = pl.ds(pl.multiple_of(c * 8, 8), 8)
    own_rows = pl.ds(pl.multiple_of(d * n, n), n)
    sib_rows = pl.ds(pl.multiple_of(sib * n, n), n)

    def at_y(j):
        return (((y + j) % 4 * 4 + zh) * 2 + core, c)

    def at_z(j):
        return ((y * 4 + (zh + j) % 4) * 2 + core, c)

    def centre_of(dx, dz):
        return (x + dx) % 4 * 2 + (zl + dz) % 2

    def remote(src, dst, send, recv, to):
        return pltpu.make_async_remote_copy(
            src_ref=src, dst_ref=dst, send_sem=send, recv_sem=recv, device_id=to, device_id_type=MESH
        )

    def got(like, sem):
        remote(like, like, sem, sem, (sib, c)).wait_recv()

    def sent(like, sem):
        remote(like, like, sem, sem, (sib, c)).wait_send()

    def block_loads(b):
        owner = ((y + b // 4) % 4 * 4 + (zh + b % 4) % 4) * 2 + core
        at = pl.ds(pl.multiple_of(owner * n, n), n)
        to = pl.ds(pl.multiple_of(b * n, n), n)
        return (
            pltpu.make_async_copy(centres.at[at], cen.at[to], loc_sem.at[4 + b]),
            pltpu.make_async_copy(coefs.at[:, at], cof.at[:, to], loc_sem.at[20 + b]),
        )

    smp_load = pltpu.make_async_copy(samples, smp.at[0], loc_sem.at[0])
    late_loads = (
        pltpu.make_async_copy(targets, tgt, loc_sem.at[1]),
        pltpu.make_async_copy(centres.at[own_rows], rows.at[0, 0], loc_sem.at[2]),
        pltpu.make_async_copy(centres.at[sib_rows], rows.at[0, 1], loc_sem.at[3]),
    )
    smp_load.start()

    @functools.partial(loop, 0, 16)
    def _(b):
        for copy in block_loads(b):
            copy.start()

    for copy in late_loads:
        copy.start()

    barrier = pltpu.get_barrier_semaphore()
    partners = [(sib, c)] + [at_y(j) for j in (1, 2, 3)] + [at_z(j) for j in (1, 2, 3)]
    for dx, dz in PAIRS[1:]:
        partners += [(d, centre_of(dx, dz)), (sib, centre_of(dx, dz))]
    for to in partners:
        pl.semaphore_signal(barrier, inc=1, device_id=to, device_id_type=MESH)

    def send_rows(pairs):
        for dx, dz in pairs:
            j = PLACE[((4 - dx) % 4, dz)]
            remote(
                cen.at[pl.ds(0, n)], rows.at[j, 0], row_send.at[PLACE[(dx, dz)]], row_recv.at[j], (d, centre_of(dx, dz))
            ).start()

    def relay_rows(dz):
        far = PLACE[(2, dz)]
        for i, (back, on) in enumerate(((1, 3), (3, 1))):
            half = pl.ds(i * 64, 64)
            remote(
                rows.at[PLACE[(back, dz)], 0, half], rows.at[far, 0, half],
                rel_send.at[dz * 2 + i], rel_recv.at[dz * 2 + i], (d, centre_of(on, 0)),
            ).start()

    def await_relayed(dz):
        for i in (0, 1):
            got(rows.at[PLACE[(2, dz)], 0, pl.ds(i * 64, 64)], rel_recv.at[dz * 2 + i])

    def forward_rows(j):
        remote(rows.at[j, 0], rows.at[j, 1], fwd_send.at[j], fwd_recv.at[j], (sib, c)).start()

    def pass_on(pairs, dz):
        for pair in pairs:
            got(rows.at[PLACE[pair], 0], row_recv.at[PLACE[pair]])
        relay_rows(dz)
        for pair in pairs:
            forward_rows(PLACE[pair])

    def norm_of(v):
        total = jnp.sum(v * v, axis=1, keepdims=True) * SCALE_SQ
        return jnp.broadcast_to(total, (n, n))

    def prepare_samples(half):
        @functools.partial(loop, 0, 4)
        def _(i):
            at = pl.ds(pl.multiple_of(i * n, n), n)
            to = pl.ds(pl.multiple_of(half * 512 + i * n, n), n)
            v = smp[half, at, :]
            hi, lo = halves(v * (-2.0 * SCALE_SQ))
            s3[to, 0:512] = hi
            s3[to, 512:1024] = hi
            s3[to, 1024:1536] = lo
            scol[to, :] = norm_of(v) + EPS

    smp_load.wait()
    prepare_samples(0)

    @functools.partial(loop, 0, 16)
    def _(b):
        for copy in block_loads(b):
            copy.wait()
        at = pl.ds(pl.multiple_of(b * n, n), n)
        v = cen[at, :]
        hi, lo = halves(v)
        c3[at, 0:512] = hi
        c3[at, 512:1024] = lo
        c3[at, 1024:1536] = hi
        norms = norm_of(v)
        ccol[at, :] = norms + EPS
        crow[:, at] = norms.T[0:8, :]
        w = cof[:, at]
        whi = w.astype(bf16).astype(f32)
        cof2[at, :] = jnp.concatenate([whi, w - whi], axis=0).T.astype(bf16)

    tn = 1024
    pacc[...] = jnp.zeros_like(pacc)

    @functools.partial(loop, 0, 4)
    def _(i):
        @pl.when(i == 1)
        def _():
            pl.semaphore_wait(barrier, len(partners))
            for k in range(4):
                at = pl.ds(k * n, n)
                remote(smp.at[0, at], smp.at[1, at], smp_send.at[k], smp_recv.at[k], (sib, c)).start()
            send_rows(FIRST_ROWS)

        @pl.when(i == 2)
        def _():
            for k in range(4):
                got(smp.at[1, pl.ds(k * n, n)], smp_recv.at[k])
            prepare_samples(1)

        these = pl.ds(pl.multiple_of(i // 2 * 512, 512), 512)
        at = pl.ds(pl.multiple_of(i % 2 * tn, tn), tn)
        cross = lax.dot_general(s3[these, :], c3[at, :], NT, preferred_element_type=f32)
        value = kernel_of(cross + lanes(scol[these, :], tn // n) + crow[0:1, at])
        hi, lo = halves(value)
        kh[these, at] = hi
        kl[these, at] = lo
        w = cof2[at, :]
        pacc[these, :] += jnp.dot(hi, w, preferred_element_type=f32) + jnp.dot(lo, w, preferred_element_type=f32)

    both = pacc[...].T
    pred[...] = both[0:64] + both[64:128]

    def member(s):
        dx, dz, kk = s // 4, s // 2 % 2, s % 2
        return centre_of(dx, dz), d + kk * (sib - d), kk

    @functools.partial(loop, 1, 16)
    def _(s):
        to, at_d, kk = member(s)
        remote(
            pred.at[pl.ds(pl.multiple_of(to * 8, 8), 8), pl.ds(pl.multiple_of(kk * 512, 512), 512)],
            pred_in.at[s - 1], p_send.at[s - 1], p_recv.at[s - 1], (at_d, to),
        ).start()

    for copy in late_loads:
        copy.wait()
    pass_on(FIRST_ROWS, 0)

    def residuals():
        loop(0, 15, lambda s: got(pred_in.at[s], p_recv.at[s]))
        total = pred[mine, 0:512] - tgt[mine, :]
        for s in range(15):
            total += pred_in[s]
        res[0, mine, :] = total

        @functools.partial(loop, 1, 16)
        def _(s):
            to, at_d, kk = member(s)
            remote(res.at[0, mine], res.at[kk, mine], q_send.at[s - 1], q_recv.at[s - 1], (at_d, to)).start()

        await_relayed(0)
        forward_rows(PLACE[(2, 0)])
        got(rows.at[1, 0], fwd_recv.at[1])
        got(rows.at[2, 0], fwd_recv.at[2])

    top, low = pl.ds(0, SUM_TOP), pl.ds(SUM_TOP, 64 - SUM_TOP)

    def gradients():
        loop(0, 15, lambda s: got(res.at[0, pl.ds(0, 8)], q_recv.at[s]))
        for dx in (1, 3):
            j = PLACE[(4 - dx, 1)]
            remote(
                rows.at[PLACE[(0, 1)], 0], rows.at[j, 0], row_send.at[PLACE[(dx, 1)]], row_recv.at[j],
                (d, centre_of(dx, 0)),
            ).start()
        for kk in (0, 1):
            hi, lo = halves(res[kk])
            lhs_r[0:64, kk * 512 : kk * 512 + 512] = lo
            lhs_r[64:128, kk * 512 : kk * 512 + 512] = hi

        @functools.partial(loop, 0, 4)
        def _(t):
            dy = (t + 1) % 4
            at = pl.ds(pl.multiple_of(dy * 512, 512), 512)
            a = jnp.dot(lhs_r[...], kh[:, at], preferred_element_type=f32)
            b = jnp.dot(lhs_r[64:128, :], kl[:, at], preferred_element_type=f32)
            gpart[dy] = a[0:64] + a[64:128] + b

            @pl.when(t < 3)
            def _():
                remote(gpart.at[dy, top], g_y.at[t], gy_send.at[t], gy_recv.at[t], at_y(t + 1)).start()

        for j in (1, 2, 3):
            remote(
                gpart.at[:, low, pl.ds(j * n, n)], h_z.at[j - 1], hz_send.at[j - 1], hz_recv.at[j - 1], at_z(j)
            ).start()
        res_out[...] = res[0]
        got(rows.at[3, 0], fwd_recv.at[3])
        got(rows.at[4, 0], fwd_recv.at[4])

    first, rest = pl.ds(0, TOP), pl.ds(TOP, 72 - TOP)
    start = pl.ds(0, n)

    def spread_first(it):
        for j in (1, 2, 3):
            to = 4 - j
            remote(
                whole.at[it, 0, first, start], whole.at[it, 0, first, pl.ds(to * n, n)],
                a_send.at[it, j - 1], a_recv.at[it, j - 1], at_z(j),
            ).start()
            remote(
                whole.at[it, 0, rest, start], whole.at[it, to, rest, start],
                a_send.at[it, j + 2], a_recv.at[it, j + 2], at_y(j),
            ).start()

    def spread_more(it):
        for j in (1, 2, 3):
            got(whole.at[it, 0, rest, start], a_recv.at[it, j + 2])
        for j in (1, 2, 3):
            to = 4 - j
            remote(
                whole.at[it, :, rest, start], whole.at[it, :, rest, pl.ds(to * n, n)],
                b_send.at[it, j - 1], b_recv.at[it, j - 1], at_z(j),
            ).start()
        for j in (1, 2, 3):
            got(whole.at[it, 0, first, start], a_recv.at[it, j - 1])
        for j in (1, 2, 3):
            remote(
                whole.at[it, 0, first], whole.at[it, 4 - j, first],
                b_send.at[it, j + 2], b_recv.at[it, j + 2], at_y(j),
            ).start()

    def sum_gradients():
        for j in range(3):
            got(g_y.at[j], gy_recv.at[j])
        gsum[...] = gpart[0, 0:SUM_TOP] + g_y[0] + g_y[1] + g_y[2]
        for j in (1, 2, 3):
            remote(
                gsum.at[:, pl.ds(j * n, n)], g_z.at[j - 1], gz_send.at[j - 1], gz_recv.at[j - 1], at_z(j)
            ).start()
        for j in range(3):
            got(h_z.at[j], hz_recv.at[j])
        hsum[...] = gpart[:, SUM_TOP:64, 0:n] + h_z[0] + h_z[1] + h_z[2]
        for j in (1, 2, 3):
            remote(hsum.at[j], h_y.at[j - 1], hy_send.at[j - 1], hy_recv.at[j - 1], at_y(j)).start()
        pass_on(LATER_ROWS, 1)
        for j in range(3):
            got(g_z.at[j], gz_recv.at[j])
            got(h_y.at[j], hy_recv.at[j])
        whole[0, 0, 0:SUM_TOP, 0:n] = gsum[:, 0:n] + g_z[0] + g_z[1] + g_z[2]
        whole[0, 0, SUM_TOP:64, 0:n] = hsum[0] + h_y[0] + h_y[1] + h_y[2]
        whole[0, 0, 64:72, 0:n] = jnp.zeros((8, n), f32)
        spread_first(0)
        got(rows.at[5, 0], fwd_recv.at[5])

    def spread_gradients():
        spread_more(0)
        await_relayed(1)
        forward_rows(7)
        got(rows.at[6, 0], fwd_recv.at[6])


    @functools.partial(loop, 0, 8)
    def _(j):
        for kk in (0, 1):
            v = rows[j, kk]
            hi, lo = halves(v * (-2.0 * SCALE_SQ))
            to = slice(kk * n, kk * n + n)
            r3[to, 0:512] = hi
            r3[to, 512:1024] = hi
            r3[to, 1024:1536] = lo
            rrow[:, to] = norm_of(v).T[0:8, :]
        cols = pl.ds(pl.multiple_of(j * 256, 256), 256)

        cross = lax.dot_general(c3[...], r3[...], NT, preferred_element_type=f32)
        hi, lo = halves(kernel_of(cross + lanes(ccol[...], 2) + rrow[0:1, :]))
        th[:, cols] = hi
        tl[:, cols] = lo

        pl.when(j == 0)(residuals)
        pl.when(j == 2)(gradients)
        pl.when(j == 4)(sum_gradients)
        pl.when(j == 5)(spread_gradients)

        @pl.when(j == 6)
        def _():
            got(rows.at[7, 0], fwd_recv.at[7])

    lhs_u[128:144, :] = jnp.ones((16, 512), bf16)
    part[...] = jnp.zeros_like(part)

    @functools.partial(loop, 0, 2)
    def _(it):
        @functools.partial(loop, 0, 4)
        def _(t):
            dy = near_first(t)

            @pl.when(t == 0)
            def _():
                for j in range(3):
                    got(whole.at[0, :, rest, start], b_recv.at[it, j])

            @pl.when(t > 0)
            def _():
                got(whole.at[0, 0, first], b_recv.at[it, 6 - dy])

            hi, lo = halves(whole[it, dy, 0:64, :])
            lhs_u[0:64, :] = lo
            lhs_u[64:128, :] = hi
            k = pl.ds(pl.multiple_of(dy * 512, 512), 512)

            @functools.partial(loop, 0, 4)
            def _(back):
                i = 3 - back
                at = pl.ds(pl.multiple_of(i * 512, 512), 512)
                a = jnp.dot(lhs_u[...], th[k, at], preferred_element_type=f32)
                b = jnp.dot(lhs_u[64:144, :], tl[k, at], preferred_element_type=f32)
                part[it, 0:64, at] += a[0:64] + a[64:128] + b[0:64]
                part[it, 64:72, at] += a[128:136] + b[64:72]

                @pl.when(t == 3)
                def _():
                    @pl.when(it == 1)
                    def _():
                        largest = whole[1, 0, 64:72, 0:n]
                        for e in range(1, 16):
                            largest = jnp.maximum(largest, whole[1, e // 4, 64:72, e % 4 * n : e % 4 * n + n])
                        largest = lanes(largest, 4)
                        part[1, 64:72, at] = largest

                    for j in (2 * i + 1, 2 * i):
                        theirs = pl.ds(pl.multiple_of((2 * j + 1) * n, n), n)
                        remote(
                            part.at[it, :, theirs], other.at[it, j], c_send.at[it, j], c_recv.at[it, j], (sib, c)
                        ).start()

        def added(a, b):
            return jnp.concatenate([a[0:64] + b[0:64], jnp.where(it == 1, jnp.maximum(a[64:72], b[64:72]), a[64:72] + b[64:72])])

        @functools.partial(loop, 0, 8)
        def _(back):
            j = 7 - back
            got(other.at[0, 0], c_recv.at[it, j])
            ours = pl.ds(pl.multiple_of(2 * j * n, n), n)
            summed[it, j] = added(part[it, :, ours], other[it, j])

            @pl.when(j > 0)
            def _():
                to = centre_of(near_first(j % 4), j // 4)
                remote(
                    summed.at[it, j], arrived.at[it, j - 1], o_send.at[it, j - 1], o_recv.at[it, j - 1], (d, to)
                ).start()

        loop(0, 7, lambda s: got(arrived.at[0, 0], o_recv.at[it, s]))
        total = summed[it, 0]
        for s in range(7):
            total = added(total, arrived[it, s])

        @pl.when(it == 0)
        def _():
            whole[1, 0, 0:64, 0:n] = total[0:64]
            whole[1, 0, 64:72, 0:n] = jnp.broadcast_to(jnp.max(total[64:72], axis=1, keepdims=True), (8, n))
            spread_first(1)
            spread_more(1)

        @pl.when(it == 1)
        def _():
            size = jnp.concatenate([1.0 / total[64:72]] * 8, axis=0)
            once, grad = whole[1, 0, 0:64, 0:n], whole[0, 0, 0:64, 0:n]
            theta = size * (3.0 * grad - size * (3.0 * once - size * total[0:64]))
            new_out[...] = cof[:, 0:n] - LEARNING_RATE * theta

    for i in range(4):
        sent(smp.at[0, pl.ds(0, n)], smp_send.at[i])
        sent(rows.at[0, 0, pl.ds(0, 64)], rel_send.at[i])
    for pair in FIRST_ROWS + LATER_ROWS:
        sent(rows.at[0, 0], row_send.at[PLACE[pair]])
    loop(1, 8, lambda j: sent(rows.at[0, 0], fwd_send.at[j]))

    @functools.partial(loop, 0, 15)
    def _(s):
        sent(pred_in.at[0], p_send.at[s])
        sent(pred_in.at[0], q_send.at[s])

    @functools.partial(loop, 0, 3)
    def _(j):
        sent(g_y.at[0], gy_send.at[j])
        sent(g_z.at[0], gz_send.at[j])
        sent(h_z.at[0], hz_send.at[j])
        sent(h_y.at[0], hy_send.at[j])
        for it in (0, 1):
            sent(whole.at[0, 0, first, start], a_send.at[it, j])
            sent(whole.at[0, 0, rest, start], a_send.at[it, j + 3])
            sent(whole.at[0, :, rest, start], b_send.at[it, j])
            sent(whole.at[0, 0, first], b_send.at[it, j + 3])

    @functools.partial(loop, 0, 8)
    def _(j):
        for it in (0, 1):
            sent(other.at[0, 0], c_send.at[it, j])

            @pl.when(j > 0)
            def _():
                sent(other.at[0, 0], o_send.at[it, j - 1])


def hand_over(res_in, new_in, res_out, new_out):
    res_out[...] = res_in[...]
    new_out[...] = new_in[...]


def body(samples, targets, centres, coefficients):
    dma = pltpu.SemaphoreType.DMA
    vmem = pltpu.VMEM
    res_t, new_t = pl.pallas_call(
        step_kernel,
        out_shape=(jax.ShapeDtypeStruct((64, 512), f32), jax.ShapeDtypeStruct((64, 128), f32)),
        in_specs=[pl.BlockSpec(memory_space=pl.ANY)] * 4,
        out_specs=[pl.BlockSpec(memory_space=vmem)] * 2,
        scratch_shapes=[
            vmem((2048, 512), f32), vmem((64, 2048), f32), vmem((2, 512, 512), f32), vmem((64, 512), f32),
            vmem((8, 2, 128, 512), f32),
            vmem((2048, 1536), bf16), vmem((2048, 128), f32), vmem((8, 2048), f32),
            vmem((1024, 1536), bf16), vmem((1024, 128), f32), vmem((256, 1536), bf16), vmem((8, 256), f32),
            vmem((2048, 128), bf16),
            vmem((1024, 2048), bf16), vmem((1024, 2048), bf16), vmem((2048, 2048), bf16), vmem((2048, 2048), bf16),
            vmem((1024, 128), f32), vmem((64, 1024), f32), vmem((15, 8, 512), f32), vmem((2, 64, 512), f32),
            vmem((4, 64, 512), f32), vmem((3, SUM_TOP, 512), f32), vmem((SUM_TOP, 512), f32), vmem((3, SUM_TOP, 128), f32),
            vmem((3, 4, 64 - SUM_TOP, 128), f32), vmem((4, 64 - SUM_TOP, 128), f32), vmem((3, 64 - SUM_TOP, 128), f32),
            vmem((2, 4, 72, 512), f32), vmem((2, 72, 2048), f32), vmem((2, 8, 72, 128), f32), vmem((2, 8, 72, 128), f32),
            vmem((2, 7, 72, 128), f32), vmem((128, 1024), bf16), vmem((144, 512), bf16),
            dma((36,)), dma((4,)), dma((4,)), dma((8,)), dma((8,)), dma((8,)), dma((8,)), dma((4,)), dma((4,)),
            dma((15,)), dma((15,)), dma((15,)), dma((15,)),
            dma((3,)), dma((3,)), dma((3,)), dma((3,)), dma((3,)), dma((3,)), dma((3,)), dma((3,)),
            dma((2, 6)), dma((2, 6)), dma((2, 6)), dma((2, 6)),
            dma((2, 8)), dma((2, 8)), dma((2, 7)), dma((2, 7)),
        ],
        compiler_params=pltpu.CompilerParams(
            collective_id=0, has_side_effects=True, vmem_limit_bytes=63 * 2**20
        ),
    )(samples, targets.T, centres, coefficients.T)
    res_t, new_t = pl.pallas_call(
        hand_over,
        out_shape=(jax.ShapeDtypeStruct((64, 512), f32), jax.ShapeDtypeStruct((64, 128), f32)),
        in_specs=[pl.BlockSpec(memory_space=vmem)] * 2,
        out_specs=[pl.BlockSpec(memory_space=vmem)] * 2,
    )(res_t, new_t)
    return res_t.T, new_t.T


def solution(mesh):
    return jax.shard_map(
        body,
        mesh=mesh,
        in_specs=(P("dp", None), P("dp", None), P("centre", None), P("centre", None)),
        out_specs=(P("dp", None), P(("centre", "dp"), None)),
        check_vma=False,
    )
```

```python
import functools
import math

import jax
import jax.numpy as jnp
from jax import lax
from jax.experimental import pallas as pl
from jax.experimental.pallas import tpu as pltpu
from jax.sharding import PartitionSpec as P

MESH = pl.DeviceIdType.MESH
f32, bf16 = jnp.float32, jnp.bfloat16
NT = (((1,), (1,)), ((), ()))

SOFTENING = 0.01
KERNEL_SCALE = 0.2
LEARNING_RATE = 4.0
SCALE_SQ = (math.log2(math.e) / KERNEL_SCALE) ** 2
EPS = SOFTENING * SCALE_SQ

PAIRS = ((0, 0), (1, 0), (3, 0), (2, 0), (0, 1), (1, 1), (3, 1), (2, 1))
PLACE = {pair: at for at, pair in enumerate(PAIRS)}
FIRST_ROWS = ((1, 0), (3, 0), (0, 1))
LATER_ROWS = ((1, 1), (3, 1))
SUM_TOP = 40
TOP = 48


def halves(x):
    hi = x.astype(bf16)
    lo = (x - hi.astype(f32)).astype(bf16)
    return hi, lo


def kernel_of(z):
    z = jnp.maximum(z, EPS)
    return jnp.exp2(-(z * lax.rsqrt(z)))


def lanes(x, times):
    return jnp.concatenate([x] * times, axis=1)


def near_first(t):
    return t + t // 2 - 2 * (t // 3)


def loop(start, stop, f):
    def step(i, _):
        f(i)
        return 0

    lax.fori_loop(start, stop, step, 0)


def step_kernel(
    samples, targets, centres, coefs, res_out, new_out,
    cen, cof, smp, tgt, rows,
    c3, ccol, crow, s3, scol, r3, rrow, cof2,
    kh, kl, th, tl,
    pacc, pred, pred_in, res,
    gpart, g_y, gsum, g_z, h_z, hsum, h_y,
    whole, part, other, summed, arrived, lhs_r, lhs_u,
    loc_sem, smp_send, smp_recv, row_send, row_recv, fwd_send, fwd_recv, rel_send, rel_recv,
    p_send, p_recv, q_send, q_recv,
    gy_send, gy_recv, gz_send, gz_recv, hz_send, hz_recv, hy_send, hy_recv,
    a_send, a_recv, b_send, b_recv, c_send, c_recv, o_send, o_recv,
):
    n = 128
    d, c = lax.axis_index("dp"), lax.axis_index("centre")
    core, zh, y = d % 2, (d // 2) % 4, d // 8
    x, zl = c // 2, c % 2
    sib = d + 1 - 2 * core
    mine = pl.ds(pl.multiple_of(c * 8, 8), 8)
    own_rows = pl.ds(pl.multiple_of(d * n, n), n)
    sib_rows = pl.ds(pl.multiple_of(sib * n, n), n)

    def at_y(j):
        return (((y + j) % 4 * 4 + zh) * 2 + core, c)

    def at_z(j):
        return ((y * 4 + (zh + j) % 4) * 2 + core, c)

    def centre_of(dx, dz):
        return (x + dx) % 4 * 2 + (zl + dz) % 2

    def remote(src, dst, send, recv, to):
        return pltpu.make_async_remote_copy(
            src_ref=src, dst_ref=dst, send_sem=send, recv_sem=recv, device_id=to, device_id_type=MESH
        )

    def got(like, sem):
        remote(like, like, sem, sem, (sib, c)).wait_recv()

    def sent(like, sem):
        remote(like, like, sem, sem, (sib, c)).wait_send()

    def block_loads(b):
        owner = ((y + b // 4) % 4 * 4 + (zh + b % 4) % 4) * 2 + core
        at = pl.ds(pl.multiple_of(owner * n, n), n)
        to = pl.ds(pl.multiple_of(b * n, n), n)
        return (
            pltpu.make_async_copy(centres.at[at], cen.at[to], loc_sem.at[4 + b]),
            pltpu.make_async_copy(coefs.at[:, at], cof.at[:, to], loc_sem.at[20 + b]),
        )

    smp_load = pltpu.make_async_copy(samples, smp.at[0], loc_sem.at[0])
    late_loads = (
        pltpu.make_async_copy(targets, tgt, loc_sem.at[1]),
        pltpu.make_async_copy(centres.at[own_rows], rows.at[0, 0], loc_sem.at[2]),
        pltpu.make_async_copy(centres.at[sib_rows], rows.at[0, 1], loc_sem.at[3]),
    )
    smp_load.start()

    @functools.partial(loop, 0, 16)
    def _(b):
        for copy in block_loads(b):
            copy.start()

    for copy in late_loads:
        copy.start()

    barrier = pltpu.get_barrier_semaphore()
    partners = [(sib, c)] + [at_y(j) for j in (1, 2, 3)] + [at_z(j) for j in (1, 2, 3)]
    for dx, dz in PAIRS[1:]:
        partners += [(d, centre_of(dx, dz)), (sib, centre_of(dx, dz))]
    for to in partners:
        pl.semaphore_signal(barrier, inc=1, device_id=to, device_id_type=MESH)

    def send_rows(pairs):
        for dx, dz in pairs:
            j = PLACE[((4 - dx) % 4, dz)]
            remote(
                cen.at[pl.ds(0, n)], rows.at[j, 0], row_send.at[PLACE[(dx, dz)]], row_recv.at[j], (d, centre_of(dx, dz))
            ).start()

    def relay_rows(dz):
        far = PLACE[(2, dz)]
        for i, (back, on) in enumerate(((1, 3), (3, 1))):
            half = pl.ds(i * 64, 64)
            remote(
                rows.at[PLACE[(back, dz)], 0, half], rows.at[far, 0, half],
                rel_send.at[dz * 2 + i], rel_recv.at[dz * 2 + i], (d, centre_of(on, 0)),
            ).start()

    def await_relayed(dz):
        for i in (0, 1):
            got(rows.at[PLACE[(2, dz)], 0, pl.ds(i * 64, 64)], rel_recv.at[dz * 2 + i])

    def forward_rows(j):
        remote(rows.at[j, 0], rows.at[j, 1], fwd_send.at[j], fwd_recv.at[j], (sib, c)).start()

    def pass_on(pairs, dz):
        for pair in pairs:
            got(rows.at[PLACE[pair], 0], row_recv.at[PLACE[pair]])
        relay_rows(dz)
        for pair in pairs:
            forward_rows(PLACE[pair])

    def norm_of(v):
        total = jnp.sum(v * v, axis=1, keepdims=True) * SCALE_SQ
        return jnp.broadcast_to(total, (n, n))

    def prepare_samples(half):
        @functools.partial(loop, 0, 4)
        def _(i):
            at = pl.ds(pl.multiple_of(i * n, n), n)
            to = pl.ds(pl.multiple_of(half * 512 + i * n, n), n)
            v = smp[half, at, :]
            hi, lo = halves(v * (-2.0 * SCALE_SQ))
            s3[to, 0:512] = hi
            s3[to, 512:1024] = hi
            s3[to, 1024:1536] = lo
            scol[to, :] = norm_of(v) + EPS

    smp_load.wait()
    prepare_samples(0)

    @functools.partial(loop, 0, 16)
    def _(b):
        for copy in block_loads(b):
            copy.wait()
        at = pl.ds(pl.multiple_of(b * n, n), n)
        v = cen[at, :]
        hi, lo = halves(v)
        c3[at, 0:512] = hi
        c3[at, 512:1024] = lo
        c3[at, 1024:1536] = hi
        norms = norm_of(v)
        ccol[at, :] = norms + EPS
        crow[:, at] = norms.T[0:8, :]
        w = cof[:, at]
        whi = w.astype(bf16).astype(f32)
        cof2[at, :] = jnp.concatenate([whi, w - whi], axis=0).T.astype(bf16)

    def member(s):
        dx, dz, kk = s // 4, s // 2 % 2, s % 2
        return centre_of(dx, dz), d + kk * (sib - d), kk

    def send_predictions(kk):
        both = pacc[kk * 512 : kk * 512 + 512, :].T
        pred[kk] = both[0:64] + both[64:128]

        @functools.partial(loop, 1 - kk, 8)
        def _(half):
            s = 2 * half + kk
            to, at_d, _ = member(s)
            remote(
                pred.at[kk, pl.ds(pl.multiple_of(to * 8, 8), 8)],
                pred_in.at[s - 1], p_send.at[s - 1], p_recv.at[s - 1], (at_d, to),
            ).start()

    tn = 1024
    pacc[...] = jnp.zeros_like(pacc)

    @functools.partial(loop, 0, 4)
    def _(i):
        @pl.when(i == 1)
        def _():
            pl.semaphore_wait(barrier, len(partners))
            for k in range(4):
                at = pl.ds(k * n, n)
                remote(smp.at[0, at], smp.at[1, at], smp_send.at[k], smp_recv.at[k], (sib, c)).start()
            send_rows(FIRST_ROWS)

        @pl.when(i == 2)
        def _():
            for k in range(4):
                got(smp.at[1, pl.ds(k * n, n)], smp_recv.at[k])
            prepare_samples(1)
            send_predictions(0)

        these = pl.ds(pl.multiple_of(i // 2 * 512, 512), 512)
        at = pl.ds(pl.multiple_of(i % 2 * tn, tn), tn)
        cross = lax.dot_general(s3[these, :], c3[at, :], NT, preferred_element_type=f32)
        value = kernel_of(cross + lanes(scol[these, :], tn // n) + crow[0:1, at])
        hi, lo = halves(value)
        kh[these, at] = hi
        kl[these, at] = lo
        w = cof2[at, :]
        pacc[these, :] += jnp.dot(hi, w, preferred_element_type=f32) + jnp.dot(lo, w, preferred_element_type=f32)

    send_predictions(1)
    for copy in late_loads:
        copy.wait()
    pass_on(FIRST_ROWS, 0)

    def residuals():
        loop(0, 15, lambda s: got(pred_in.at[s], p_recv.at[s]))
        total = pred[0, mine, :] - tgt[mine, :]
        for s in range(15):
            total += pred_in[s]
        res[0, mine, :] = total

        @functools.partial(loop, 1, 16)
        def _(s):
            to, at_d, kk = member(s)
            remote(res.at[0, mine], res.at[kk, mine], q_send.at[s - 1], q_recv.at[s - 1], (at_d, to)).start()

        for dx in (1, 3):
            j = PLACE[(4 - dx, 1)]
            remote(
                rows.at[PLACE[(0, 1)], 0], rows.at[j, 0], row_send.at[PLACE[(dx, 1)]], row_recv.at[j],
                (d, centre_of(dx, 0)),
            ).start()
        await_relayed(0)
        forward_rows(PLACE[(2, 0)])
        got(rows.at[1, 0], fwd_recv.at[1])
        got(rows.at[2, 0], fwd_recv.at[2])

    top, low = pl.ds(0, SUM_TOP), pl.ds(SUM_TOP, 64 - SUM_TOP)

    def gradients():
        loop(0, 15, lambda s: got(res.at[0, pl.ds(0, 8)], q_recv.at[s]))
        for kk in (0, 1):
            hi, lo = halves(res[kk])
            lhs_r[0:64, kk * 512 : kk * 512 + 512] = lo
            lhs_r[64:128, kk * 512 : kk * 512 + 512] = hi

        @functools.partial(loop, 0, 4)
        def _(t):
            dy = (t + 1) % 4
            at = pl.ds(pl.multiple_of(dy * 512, 512), 512)
            a = jnp.dot(lhs_r[...], kh[:, at], preferred_element_type=f32)
            b = jnp.dot(lhs_r[64:128, :], kl[:, at], preferred_element_type=f32)
            gpart[dy] = a[0:64] + a[64:128] + b

            @pl.when(t < 3)
            def _():
                remote(gpart.at[dy, top], g_y.at[t], gy_send.at[t], gy_recv.at[t], at_y(t + 1)).start()

        for j in (1, 2, 3):
            remote(
                gpart.at[:, low, pl.ds(j * n, n)], h_z.at[j - 1], hz_send.at[j - 1], hz_recv.at[j - 1], at_z(j)
            ).start()
        res_out[...] = res[0]
        got(rows.at[3, 0], fwd_recv.at[3])
        got(rows.at[4, 0], fwd_recv.at[4])

    first, rest = pl.ds(0, TOP), pl.ds(TOP, 72 - TOP)
    start = pl.ds(0, n)

    def spread_first(it):
        for j in (1, 2, 3):
            to = 4 - j
            remote(
                whole.at[it, 0, first, start], whole.at[it, 0, first, pl.ds(to * n, n)],
                a_send.at[it, j - 1], a_recv.at[it, j - 1], at_z(j),
            ).start()
            remote(
                whole.at[it, 0, rest, start], whole.at[it, to, rest, start],
                a_send.at[it, j + 2], a_recv.at[it, j + 2], at_y(j),
            ).start()

    def spread_more(it):
        for j in (1, 2, 3):
            got(whole.at[it, 0, rest, start], a_recv.at[it, j + 2])
        for j in (1, 2, 3):
            to = 4 - j
            remote(
                whole.at[it, :, rest, start], whole.at[it, :, rest, pl.ds(to * n, n)],
                b_send.at[it, j - 1], b_recv.at[it, j - 1], at_z(j),
            ).start()
        for j in (1, 2, 3):
            got(whole.at[it, 0, first, start], a_recv.at[it, j - 1])
        for j in (1, 2, 3):
            remote(
                whole.at[it, 0, first], whole.at[it, 4 - j, first],
                b_send.at[it, j + 2], b_recv.at[it, j + 2], at_y(j),
            ).start()

    def sum_gradients():
        for j in range(3):
            got(g_y.at[j], gy_recv.at[j])
        gsum[...] = gpart[0, 0:SUM_TOP] + g_y[0] + g_y[1] + g_y[2]
        for j in (1, 2, 3):
            remote(
                gsum.at[:, pl.ds(j * n, n)], g_z.at[j - 1], gz_send.at[j - 1], gz_recv.at[j - 1], at_z(j)
            ).start()
        for j in range(3):
            got(h_z.at[j], hz_recv.at[j])
        hsum[...] = gpart[:, SUM_TOP:64, 0:n] + h_z[0] + h_z[1] + h_z[2]
        for j in (1, 2, 3):
            remote(hsum.at[j], h_y.at[j - 1], hy_send.at[j - 1], hy_recv.at[j - 1], at_y(j)).start()
        for j in range(3):
            got(g_z.at[j], gz_recv.at[j])
            got(h_y.at[j], hy_recv.at[j])
        whole[0, 0, 0:SUM_TOP, 0:n] = gsum[:, 0:n] + g_z[0] + g_z[1] + g_z[2]
        whole[0, 0, SUM_TOP:64, 0:n] = hsum[0] + h_y[0] + h_y[1] + h_y[2]
        whole[0, 0, 64:72, 0:n] = jnp.zeros((8, n), f32)
        spread_first(0)
        got(rows.at[5, 0], fwd_recv.at[5])

    def spread_gradients():
        spread_more(0)
        await_relayed(1)
        forward_rows(7)
        got(rows.at[6, 0], fwd_recv.at[6])


    @functools.partial(loop, 0, 8)
    def _(j):
        for kk in (0, 1):
            v = rows[j, kk]
            hi, lo = halves(v * (-2.0 * SCALE_SQ))
            to = slice(kk * n, kk * n + n)
            r3[to, 0:512] = hi
            r3[to, 512:1024] = hi
            r3[to, 1024:1536] = lo
            rrow[:, to] = norm_of(v).T[0:8, :]
        cols = pl.ds(pl.multiple_of(j * 256, 256), 256)

        cross = lax.dot_general(c3[...], r3[...], NT, preferred_element_type=f32)
        hi, lo = halves(kernel_of(cross + lanes(ccol[...], 2) + rrow[0:1, :]))
        th[:, cols] = hi
        tl[:, cols] = lo

        pl.when(j == 0)(residuals)
        pl.when(j == 2)(gradients)

        @pl.when(j == 3)
        def _():
            pass_on(LATER_ROWS, 1)

        pl.when(j == 4)(sum_gradients)
        pl.when(j == 5)(spread_gradients)

        @pl.when(j == 6)
        def _():
            got(rows.at[7, 0], fwd_recv.at[7])

    lhs_u[128:144, :] = jnp.ones((16, 512), bf16)
    part[...] = jnp.zeros_like(part)

    @functools.partial(loop, 0, 2)
    def _(it):
        @functools.partial(loop, 0, 4)
        def _(t):
            dy = near_first(t)

            @pl.when(t == 0)
            def _():
                for j in range(3):
                    got(whole.at[0, :, rest, start], b_recv.at[it, j])

            @pl.when(t > 0)
            def _():
                got(whole.at[0, 0, first], b_recv.at[it, 6 - dy])

            hi, lo = halves(whole[it, dy, 0:64, :])
            lhs_u[0:64, :] = lo
            lhs_u[64:128, :] = hi
            k = pl.ds(pl.multiple_of(dy * 512, 512), 512)

            @functools.partial(loop, 0, 4)
            def _(back):
                i = 3 - back
                at = pl.ds(pl.multiple_of(i * 512, 512), 512)
                a = jnp.dot(lhs_u[...], th[k, at], preferred_element_type=f32)
                b = jnp.dot(lhs_u[64:144, :], tl[k, at], preferred_element_type=f32)
                part[it, 0:64, at] += a[0:64] + a[64:128] + b[0:64]
                part[it, 64:72, at] += a[128:136] + b[64:72]

                @pl.when(t == 3)
                def _():
                    @pl.when(it == 1)
                    def _():
                        largest = whole[1, 0, 64:72, 0:n]
                        for e in range(1, 16):
                            largest = jnp.maximum(largest, whole[1, e // 4, 64:72, e % 4 * n : e % 4 * n + n])
                        largest = lanes(largest, 4)
                        part[1, 64:72, at] = largest

                    for j in (2 * i + 1, 2 * i):
                        theirs = pl.ds(pl.multiple_of((2 * j + 1) * n, n), n)
                        remote(
                            part.at[it, :, theirs], other.at[it, j], c_send.at[it, j], c_recv.at[it, j], (sib, c)
                        ).start()

        def added(a, b):
            return jnp.concatenate([a[0:64] + b[0:64], jnp.where(it == 1, jnp.maximum(a[64:72], b[64:72]), a[64:72] + b[64:72])])

        @functools.partial(loop, 0, 8)
        def _(back):
            j = 7 - back
            got(other.at[0, 0], c_recv.at[it, j])
            ours = pl.ds(pl.multiple_of(2 * j * n, n), n)
            summed[it, j] = added(part[it, :, ours], other[it, j])

            @pl.when(j > 0)
            def _():
                to = centre_of(near_first(j % 4), j // 4)
                remote(
                    summed.at[it, j], arrived.at[it, j - 1], o_send.at[it, j - 1], o_recv.at[it, j - 1], (d, to)
                ).start()

        loop(0, 7, lambda s: got(arrived.at[0, 0], o_recv.at[it, s]))
        total = summed[it, 0]
        for s in range(7):
            total = added(total, arrived[it, s])

        @pl.when(it == 0)
        def _():
            whole[1, 0, 0:64, 0:n] = total[0:64]
            whole[1, 0, 64:72, 0:n] = jnp.broadcast_to(jnp.max(total[64:72], axis=1, keepdims=True), (8, n))
            spread_first(1)
            spread_more(1)

        @pl.when(it == 1)
        def _():
            size = jnp.concatenate([1.0 / total[64:72]] * 8, axis=0)
            once, grad = whole[1, 0, 0:64, 0:n], whole[0, 0, 0:64, 0:n]
            theta = size * (3.0 * grad - size * (3.0 * once - size * total[0:64]))
            new_out[...] = cof[:, 0:n] - LEARNING_RATE * theta

    for i in range(4):
        sent(smp.at[0, pl.ds(0, n)], smp_send.at[i])
        sent(rows.at[0, 0, pl.ds(0, 64)], rel_send.at[i])
    for pair in FIRST_ROWS + LATER_ROWS:
        sent(rows.at[0, 0], row_send.at[PLACE[pair]])
    loop(1, 8, lambda j: sent(rows.at[0, 0], fwd_send.at[j]))

    @functools.partial(loop, 0, 15)
    def _(s):
        sent(pred_in.at[0], p_send.at[s])
        sent(pred_in.at[0], q_send.at[s])

    @functools.partial(loop, 0, 3)
    def _(j):
        sent(g_y.at[0], gy_send.at[j])
        sent(g_z.at[0], gz_send.at[j])
        sent(h_z.at[0], hz_send.at[j])
        sent(h_y.at[0], hy_send.at[j])
        for it in (0, 1):
            sent(whole.at[0, 0, first, start], a_send.at[it, j])
            sent(whole.at[0, 0, rest, start], a_send.at[it, j + 3])
            sent(whole.at[0, :, rest, start], b_send.at[it, j])
            sent(whole.at[0, 0, first], b_send.at[it, j + 3])

    @functools.partial(loop, 0, 8)
    def _(j):
        for it in (0, 1):
            sent(other.at[0, 0], c_send.at[it, j])

            @pl.when(j > 0)
            def _():
                sent(other.at[0, 0], o_send.at[it, j - 1])


def hand_over(res_in, new_in, res_out, new_out):
    res_out[...] = res_in[...]
    new_out[...] = new_in[...]


def body(samples, targets, centres, coefficients):
    dma = pltpu.SemaphoreType.DMA
    vmem = pltpu.VMEM
    res_t, new_t = pl.pallas_call(
        step_kernel,
        out_shape=(jax.ShapeDtypeStruct((64, 512), f32), jax.ShapeDtypeStruct((64, 128), f32)),
        in_specs=[pl.BlockSpec(memory_space=pl.ANY)] * 4,
        out_specs=[pl.BlockSpec(memory_space=vmem)] * 2,
        scratch_shapes=[
            vmem((2048, 512), f32), vmem((64, 2048), f32), vmem((2, 512, 512), f32), vmem((64, 512), f32),
            vmem((8, 2, 128, 512), f32),
            vmem((2048, 1536), bf16), vmem((2048, 128), f32), vmem((8, 2048), f32),
            vmem((1024, 1536), bf16), vmem((1024, 128), f32), vmem((256, 1536), bf16), vmem((8, 256), f32),
            vmem((2048, 128), bf16),
            vmem((1024, 2048), bf16), vmem((1024, 2048), bf16), vmem((2048, 2048), bf16), vmem((2048, 2048), bf16),
            vmem((1024, 128), f32), vmem((2, 64, 512), f32), vmem((15, 8, 512), f32), vmem((2, 64, 512), f32),
            vmem((4, 64, 512), f32), vmem((3, SUM_TOP, 512), f32), vmem((SUM_TOP, 512), f32), vmem((3, SUM_TOP, 128), f32),
            vmem((3, 4, 64 - SUM_TOP, 128), f32), vmem((4, 64 - SUM_TOP, 128), f32), vmem((3, 64 - SUM_TOP, 128), f32),
            vmem((2, 4, 72, 512), f32), vmem((2, 72, 2048), f32), vmem((2, 8, 72, 128), f32), vmem((2, 8, 72, 128), f32),
            vmem((2, 7, 72, 128), f32), vmem((128, 1024), bf16), vmem((144, 512), bf16),
            dma((36,)), dma((4,)), dma((4,)), dma((8,)), dma((8,)), dma((8,)), dma((8,)), dma((4,)), dma((4,)),
            dma((15,)), dma((15,)), dma((15,)), dma((15,)),
            dma((3,)), dma((3,)), dma((3,)), dma((3,)), dma((3,)), dma((3,)), dma((3,)), dma((3,)),
            dma((2, 6)), dma((2, 6)), dma((2, 6)), dma((2, 6)),
            dma((2, 8)), dma((2, 8)), dma((2, 7)), dma((2, 7)),
        ],
        compiler_params=pltpu.CompilerParams(
            collective_id=0, has_side_effects=True, vmem_limit_bytes=63 * 2**20
        ),
    )(samples, targets.T, centres, coefficients.T)
    res_t, new_t = pl.pallas_call(
        hand_over,
        out_shape=(jax.ShapeDtypeStruct((64, 512), f32), jax.ShapeDtypeStruct((64, 128), f32)),
        in_specs=[pl.BlockSpec(memory_space=vmem)] * 2,
        out_specs=[pl.BlockSpec(memory_space=vmem)] * 2,
    )(res_t, new_t)
    return res_t.T, new_t.T


def solution(mesh):
    return jax.shard_map(
        body,
        mesh=mesh,
        in_specs=(P("dp", None), P("dp", None), P("centre", None), P("centre", None)),
        out_specs=(P("dp", None), P(("centre", "dp"), None)),
        check_vma=False,
    )
```

```python
import functools
import math

import jax
import jax.numpy as jnp
from jax import lax
from jax.experimental import pallas as pl
from jax.experimental.pallas import tpu as pltpu
from jax.sharding import PartitionSpec as P

MESH = pl.DeviceIdType.MESH
f32, bf16 = jnp.float32, jnp.bfloat16
NT = (((1,), (1,)), ((), ()))

SOFTENING = 0.01
KERNEL_SCALE = 0.2
LEARNING_RATE = 4.0
SCALE_SQ = (math.log2(math.e) / KERNEL_SCALE) ** 2
EPS = SOFTENING * SCALE_SQ

PAIRS = ((0, 0), (1, 0), (3, 0), (2, 0), (0, 1), (1, 1), (3, 1), (2, 1))
PLACE = {pair: at for at, pair in enumerate(PAIRS)}
FIRST_ROWS = ((1, 0), (3, 0), (0, 1))
LATER_ROWS = ((1, 1), (3, 1))
SUM_TOP = 40
TOP = 48


def halves(x):
    hi = x.astype(bf16)
    lo = (x - hi.astype(f32)).astype(bf16)
    return hi, lo


def kernel_of(z):
    z = jnp.maximum(z, EPS)
    return jnp.exp2(-(z * lax.rsqrt(z)))


def lanes(x, times):
    return jnp.concatenate([x] * times, axis=1)


def near_first(t):
    return t + t // 2 - 2 * (t // 3)


def loop(start, stop, f):
    def step(i, _):
        f(i)
        return 0

    lax.fori_loop(start, stop, step, 0)


def step_kernel(
    samples, targets, centres, coefs, res_out, new_out,
    cen, cof, smp, tgt, rows,
    c3, ccol, crow, s3, scol, r3, rrow, cof2,
    kh, kl, th, tl,
    pacc, pred, pred_in, res,
    gpart, g_y, gsum, g_z, h_z, hsum, h_y,
    whole, part, other, summed, arrived, lhs_r, lhs_u,
    loc_sem, smp_send, smp_recv, row_send, row_recv, fwd_send, fwd_recv, rel_send, rel_recv,
    p_send, p_recv, q_send, q_recv,
    gy_send, gy_recv, gz_send, gz_recv, hz_send, hz_recv, hy_send, hy_recv,
    a_send, a_recv, b_send, b_recv, c_send, c_recv, o_send, o_recv,
):
    n = 128
    d, c = lax.axis_index("dp"), lax.axis_index("centre")
    core, zh, y = d % 2, (d // 2) % 4, d // 8
    x, zl = c // 2, c % 2
    sib = d + 1 - 2 * core
    mine = pl.ds(pl.multiple_of(c * 8, 8), 8)
    own_rows = pl.ds(pl.multiple_of(d * n, n), n)
    sib_rows = pl.ds(pl.multiple_of(sib * n, n), n)

    def at_y(j):
        return (((y + j) % 4 * 4 + zh) * 2 + core, c)

    def at_z(j):
        return ((y * 4 + (zh + j) % 4) * 2 + core, c)

    def centre_of(dx, dz):
        return (x + dx) % 4 * 2 + (zl + dz) % 2

    def remote(src, dst, send, recv, to):
        return pltpu.make_async_remote_copy(
            src_ref=src, dst_ref=dst, send_sem=send, recv_sem=recv, device_id=to, device_id_type=MESH
        )

    def got(like, sem):
        remote(like, like, sem, sem, (sib, c)).wait_recv()

    def sent(like, sem):
        remote(like, like, sem, sem, (sib, c)).wait_send()

    def block_loads(b):
        owner = ((y + b // 4) % 4 * 4 + (zh + b % 4) % 4) * 2 + core
        at = pl.ds(pl.multiple_of(owner * n, n), n)
        to = pl.ds(pl.multiple_of(b * n, n), n)
        return (
            pltpu.make_async_copy(centres.at[at], cen.at[to], loc_sem.at[4 + b]),
            pltpu.make_async_copy(coefs.at[:, at], cof.at[:, to], loc_sem.at[20 + b]),
        )

    smp_load = pltpu.make_async_copy(samples, smp.at[0], loc_sem.at[0])
    late_loads = (
        pltpu.make_async_copy(targets, tgt, loc_sem.at[1]),
        pltpu.make_async_copy(centres.at[own_rows], rows.at[0, 0], loc_sem.at[2]),
        pltpu.make_async_copy(centres.at[sib_rows], rows.at[0, 1], loc_sem.at[3]),
    )
    smp_load.start()

    @functools.partial(loop, 0, 16)
    def _(b):
        for copy in block_loads(b):
            copy.start()

    for copy in late_loads:
        copy.start()

    barrier = pltpu.get_barrier_semaphore()
    partners = [(sib, c)] + [at_y(j) for j in (1, 2, 3)] + [at_z(j) for j in (1, 2, 3)]
    for dx, dz in PAIRS[1:]:
        partners += [(d, centre_of(dx, dz)), (sib, centre_of(dx, dz))]
    for to in partners:
        pl.semaphore_signal(barrier, inc=1, device_id=to, device_id_type=MESH)

    def send_rows(pairs):
        for dx, dz in pairs:
            j = PLACE[((4 - dx) % 4, dz)]
            remote(
                cen.at[pl.ds(0, n)], rows.at[j, 0], row_send.at[PLACE[(dx, dz)]], row_recv.at[j], (d, centre_of(dx, dz))
            ).start()

    def relay_rows(dz):
        far = PLACE[(2, dz)]
        for i, (back, on) in enumerate(((1, 3), (3, 1))):
            half = pl.ds(i * 64, 64)
            remote(
                rows.at[PLACE[(back, dz)], 0, half], rows.at[far, 0, half],
                rel_send.at[dz * 2 + i], rel_recv.at[dz * 2 + i], (d, centre_of(on, 0)),
            ).start()

    def await_relayed(dz):
        for i in (0, 1):
            got(rows.at[PLACE[(2, dz)], 0, pl.ds(i * 64, 64)], rel_recv.at[dz * 2 + i])

    def forward_rows(j):
        remote(rows.at[j, 0], rows.at[j, 1], fwd_send.at[j], fwd_recv.at[j], (sib, c)).start()

    def pass_on(pairs, dz):
        for pair in pairs:
            got(rows.at[PLACE[pair], 0], row_recv.at[PLACE[pair]])
        relay_rows(dz)
        for pair in pairs:
            forward_rows(PLACE[pair])

    def norm_of(v):
        total = jnp.sum(v * v, axis=1, keepdims=True) * SCALE_SQ
        return jnp.broadcast_to(total, (n, n))

    def prepare_samples(half):
        @functools.partial(loop, 0, 4)
        def _(i):
            at = pl.ds(pl.multiple_of(i * n, n), n)
            to = pl.ds(pl.multiple_of(half * 512 + i * n, n), n)
            v = smp[half, at, :]
            hi, lo = halves(v * (-2.0 * SCALE_SQ))
            s3[to, 0:512] = hi
            s3[to, 512:1024] = hi
            s3[to, 1024:1536] = lo
            scol[to, :] = norm_of(v) + EPS

    smp_load.wait()
    prepare_samples(0)

    @functools.partial(loop, 0, 16)
    def _(b):
        for copy in block_loads(b):
            copy.wait()
        at = pl.ds(pl.multiple_of(b * n, n), n)
        v = cen[at, :]
        hi, lo = halves(v)
        c3[at, 0:512] = hi
        c3[at, 512:1024] = lo
        c3[at, 1024:1536] = hi
        norms = norm_of(v)
        ccol[at, :] = norms + EPS
        crow[:, at] = norms.T[0:8, :]
        w = cof[:, at]
        whi = w.astype(bf16).astype(f32)
        cof2[at, :] = jnp.concatenate([whi, w - whi], axis=0).T.astype(bf16)

    def member(s):
        dx, dz, kk = s // 4, s // 2 % 2, s % 2
        return centre_of(dx, dz), d + kk * (sib - d), kk

    def send_predictions(kk):
        both = pacc[kk * 512 : kk * 512 + 512, :].T
        pred[kk] = both[0:64] + both[64:128]

        @functools.partial(loop, 1 - kk, 8)
        def _(half):
            s = 2 * half + kk
            to, at_d, _ = member(s)
            remote(
                pred.at[kk, pl.ds(pl.multiple_of(to * 8, 8), 8)],
                pred_in.at[s - 1], p_send.at[s - 1], p_recv.at[s - 1], (at_d, to),
            ).start()

    tn = 1024
    pacc[...] = jnp.zeros_like(pacc)

    @functools.partial(loop, 0, 4)
    def _(i):
        @pl.when(i == 1)
        def _():
            pl.semaphore_wait(barrier, len(partners))
            for k in range(4):
                at = pl.ds(k * n, n)
                remote(smp.at[0, at], smp.at[1, at], smp_send.at[k], smp_recv.at[k], (sib, c)).start()
            send_rows(FIRST_ROWS)

        @pl.when(i == 2)
        def _():
            for k in range(4):
                got(smp.at[1, pl.ds(k * n, n)], smp_recv.at[k])
            prepare_samples(1)
            send_predictions(0)

        these = pl.ds(pl.multiple_of(i // 2 * 512, 512), 512)
        at = pl.ds(pl.multiple_of(i % 2 * tn, tn), tn)
        cross = lax.dot_general(s3[these, :], c3[at, :], NT, preferred_element_type=f32)
        value = kernel_of(cross + lanes(scol[these, :], tn // n) + crow[0:1, at])
        hi, lo = halves(value)
        kh[these, at] = hi
        kl[these, at] = lo
        w = cof2[at, :]
        pacc[these, :] += jnp.dot(hi, w, preferred_element_type=f32) + jnp.dot(lo, w, preferred_element_type=f32)

    send_predictions(1)
    for copy in late_loads:
        copy.wait()
    pass_on(FIRST_ROWS, 0)

    def residuals():
        loop(0, 15, lambda s: got(pred_in.at[s], p_recv.at[s]))
        total = pred[0, mine, :] - tgt[mine, :]
        for s in range(15):
            total += pred_in[s]
        res[0, mine, :] = total

        @functools.partial(loop, 1, 16)
        def _(s):
            to, at_d, kk = member(s)
            remote(res.at[0, mine], res.at[kk, mine], q_send.at[s - 1], q_recv.at[s - 1], (at_d, to)).start()

        for dx in (1, 3):
            j = PLACE[(4 - dx, 1)]
            remote(
                rows.at[PLACE[(0, 1)], 0], rows.at[j, 0], row_send.at[PLACE[(dx, 1)]], row_recv.at[j],
                (d, centre_of(dx, 0)),
            ).start()
        got(rows.at[1, 0], fwd_recv.at[1])
        got(rows.at[2, 0], fwd_recv.at[2])

    top, low = pl.ds(0, SUM_TOP), pl.ds(SUM_TOP, 64 - SUM_TOP)

    def gradients():
        loop(0, 15, lambda s: got(res.at[0, pl.ds(0, 8)], q_recv.at[s]))
        for kk in (0, 1):
            hi, lo = halves(res[kk])
            lhs_r[0:64, kk * 512 : kk * 512 + 512] = lo
            lhs_r[64:128, kk * 512 : kk * 512 + 512] = hi

        @functools.partial(loop, 0, 4)
        def _(t):
            dy = 2 - t + 3 * (t // 2) - 2 * (t // 3)
            at = pl.ds(pl.multiple_of(dy * 512, 512), 512)
            a = jnp.dot(lhs_r[...], kh[:, at], preferred_element_type=f32)
            b = jnp.dot(lhs_r[64:128, :], kl[:, at], preferred_element_type=f32)
            gpart[dy] = a[0:64] + a[64:128] + b

            @pl.when(t < 3)
            def _():
                remote(gpart.at[dy, top], g_y.at[dy - 1], gy_send.at[dy - 1], gy_recv.at[dy - 1], at_y(dy)).start()

        for j in (2, 1, 3):
            remote(
                gpart.at[:, low, pl.ds(j * n, n)], h_z.at[j - 1], hz_send.at[j - 1], hz_recv.at[j - 1], at_z(j)
            ).start()
        res_out[...] = res[0]
        got(rows.at[3, 0], fwd_recv.at[3])
        got(rows.at[4, 0], fwd_recv.at[4])

    first, rest = pl.ds(0, TOP), pl.ds(TOP, 72 - TOP)
    start = pl.ds(0, n)

    def spread_first(it):
        for j in (2, 1, 3):
            to = 4 - j
            remote(
                whole.at[it, 0, first, start], whole.at[it, 0, first, pl.ds(to * n, n)],
                a_send.at[it, j - 1], a_recv.at[it, j - 1], at_z(j),
            ).start()
            remote(
                whole.at[it, 0, rest, start], whole.at[it, to, rest, start],
                a_send.at[it, j + 2], a_recv.at[it, j + 2], at_y(j),
            ).start()

    def spread_more(it):
        for j in (1, 2, 3):
            got(whole.at[it, 0, rest, start], a_recv.at[it, j + 2])
        for j in (2, 1, 3):
            to = 4 - j
            remote(
                whole.at[it, :, rest, start], whole.at[it, :, rest, pl.ds(to * n, n)],
                b_send.at[it, j - 1], b_recv.at[it, j - 1], at_z(j),
            ).start()
        for j in (1, 2, 3):
            got(whole.at[it, 0, first, start], a_recv.at[it, j - 1])
        for j in (2, 1, 3):
            remote(
                whole.at[it, 0, first], whole.at[it, 4 - j, first],
                b_send.at[it, j + 2], b_recv.at[it, j + 2], at_y(j),
            ).start()

    def sum_gradients():
        for j in range(3):
            got(g_y.at[j], gy_recv.at[j])
        gsum[...] = gpart[0, 0:SUM_TOP] + g_y[0] + g_y[1] + g_y[2]
        for j in (2, 1, 3):
            remote(
                gsum.at[:, pl.ds(j * n, n)], g_z.at[j - 1], gz_send.at[j - 1], gz_recv.at[j - 1], at_z(j)
            ).start()
        for j in range(3):
            got(h_z.at[j], hz_recv.at[j])
        hsum[...] = gpart[:, SUM_TOP:64, 0:n] + h_z[0] + h_z[1] + h_z[2]
        for j in (2, 1, 3):
            remote(hsum.at[j], h_y.at[j - 1], hy_send.at[j - 1], hy_recv.at[j - 1], at_y(j)).start()
        for j in range(3):
            got(g_z.at[j], gz_recv.at[j])
            got(h_y.at[j], hy_recv.at[j])
        whole[0, 0, 0:SUM_TOP, 0:n] = gsum[:, 0:n] + g_z[0] + g_z[1] + g_z[2]
        whole[0, 0, SUM_TOP:64, 0:n] = hsum[0] + h_y[0] + h_y[1] + h_y[2]
        whole[0, 0, 64:72, 0:n] = jnp.zeros((8, n), f32)
        spread_first(0)
        got(rows.at[5, 0], fwd_recv.at[5])

    def spread_gradients():
        spread_more(0)
        await_relayed(1)
        forward_rows(7)
        got(rows.at[6, 0], fwd_recv.at[6])


    @functools.partial(loop, 0, 8)
    def _(j):
        for kk in (0, 1):
            v = rows[j, kk]
            hi, lo = halves(v * (-2.0 * SCALE_SQ))
            to = slice(kk * n, kk * n + n)
            r3[to, 0:512] = hi
            r3[to, 512:1024] = hi
            r3[to, 1024:1536] = lo
            rrow[:, to] = norm_of(v).T[0:8, :]
        cols = pl.ds(pl.multiple_of(j * 256, 256), 256)

        cross = lax.dot_general(c3[...], r3[...], NT, preferred_element_type=f32)
        hi, lo = halves(kernel_of(cross + lanes(ccol[...], 2) + rrow[0:1, :]))
        th[:, cols] = hi
        tl[:, cols] = lo

        pl.when(j == 0)(residuals)
        pl.when(j == 2)(gradients)

        @pl.when(j == 1)
        def _():
            await_relayed(0)
            forward_rows(PLACE[(2, 0)])

        @pl.when(j == 3)
        def _():
            pass_on(LATER_ROWS, 1)

        pl.when(j == 4)(sum_gradients)
        pl.when(j == 5)(spread_gradients)

        @pl.when(j == 6)
        def _():
            got(rows.at[7, 0], fwd_recv.at[7])

    lhs_u[128:144, :] = jnp.ones((16, 512), bf16)
    part[...] = jnp.zeros_like(part)

    @functools.partial(loop, 0, 2)
    def _(it):
        @functools.partial(loop, 0, 4)
        def _(t):
            dy = near_first(t)

            @pl.when(t == 0)
            def _():
                for j in range(3):
                    got(whole.at[0, :, rest, start], b_recv.at[it, j])

            @pl.when(t > 0)
            def _():
                got(whole.at[0, 0, first], b_recv.at[it, 6 - dy])

            hi, lo = halves(whole[it, dy, 0:64, :])
            lhs_u[0:64, :] = lo
            lhs_u[64:128, :] = hi
            k = pl.ds(pl.multiple_of(dy * 512, 512), 512)

            @functools.partial(loop, 0, 2)
            def _(back):
                i = 1 - back
                at = pl.ds(pl.multiple_of(i * 1024, 1024), 1024)
                a = jnp.dot(lhs_u[...], th[k, at], preferred_element_type=f32)
                b = jnp.dot(lhs_u[64:144, :], tl[k, at], preferred_element_type=f32)
                part[it, 0:64, at] += a[0:64] + a[64:128] + b[0:64]
                part[it, 64:72, at] += a[128:136] + b[64:72]

                @pl.when(t == 3)
                def _():
                    @pl.when(it == 1)
                    def _():
                        largest = whole[1, 0, 64:72, 0:n]
                        for e in range(1, 16):
                            largest = jnp.maximum(largest, whole[1, e // 4, 64:72, e % 4 * n : e % 4 * n + n])
                        largest = lanes(largest, 8)
                        part[1, 64:72, at] = largest

                    for j in (4 * i + 3, 4 * i + 2, 4 * i + 1, 4 * i):
                        theirs = pl.ds(pl.multiple_of((2 * j + 1) * n, n), n)
                        remote(
                            part.at[it, :, theirs], other.at[it, j], c_send.at[it, j], c_recv.at[it, j], (sib, c)
                        ).start()

        def added(a, b):
            return jnp.concatenate([a[0:64] + b[0:64], jnp.where(it == 1, jnp.maximum(a[64:72], b[64:72]), a[64:72] + b[64:72])])

        @functools.partial(loop, 0, 8)
        def _(back):
            j = 7 - back
            got(other.at[0, 0], c_recv.at[it, j])
            ours = pl.ds(pl.multiple_of(2 * j * n, n), n)
            summed[it, j] = added(part[it, :, ours], other[it, j])

            @pl.when(j > 0)
            def _():
                to = centre_of(near_first(j % 4), j // 4)
                remote(
                    summed.at[it, j], arrived.at[it, j - 1], o_send.at[it, j - 1], o_recv.at[it, j - 1], (d, to)
                ).start()

        loop(0, 7, lambda s: got(arrived.at[0, 0], o_recv.at[it, s]))
        total = summed[it, 0]
        for s in range(7):
            total = added(total, arrived[it, s])

        @pl.when(it == 0)
        def _():
            whole[1, 0, 0:64, 0:n] = total[0:64]
            whole[1, 0, 64:72, 0:n] = jnp.broadcast_to(jnp.max(total[64:72], axis=1, keepdims=True), (8, n))
            spread_first(1)
            spread_more(1)

        @pl.when(it == 1)
        def _():
            size = jnp.concatenate([1.0 / total[64:72]] * 8, axis=0)
            once, grad = whole[1, 0, 0:64, 0:n], whole[0, 0, 0:64, 0:n]
            theta = size * (3.0 * grad - size * (3.0 * once - size * total[0:64]))
            new_out[...] = cof[:, 0:n] - LEARNING_RATE * theta

    for i in range(4):
        sent(smp.at[0, pl.ds(0, n)], smp_send.at[i])
        sent(rows.at[0, 0, pl.ds(0, 64)], rel_send.at[i])
    for pair in FIRST_ROWS + LATER_ROWS:
        sent(rows.at[0, 0], row_send.at[PLACE[pair]])
    loop(1, 8, lambda j: sent(rows.at[0, 0], fwd_send.at[j]))

    @functools.partial(loop, 0, 15)
    def _(s):
        sent(pred_in.at[0], p_send.at[s])
        sent(pred_in.at[0], q_send.at[s])

    @functools.partial(loop, 0, 3)
    def _(j):
        sent(g_y.at[0], gy_send.at[j])
        sent(g_z.at[0], gz_send.at[j])
        sent(h_z.at[0], hz_send.at[j])
        sent(h_y.at[0], hy_send.at[j])
        for it in (0, 1):
            sent(whole.at[0, 0, first, start], a_send.at[it, j])
            sent(whole.at[0, 0, rest, start], a_send.at[it, j + 3])
            sent(whole.at[0, :, rest, start], b_send.at[it, j])
            sent(whole.at[0, 0, first], b_send.at[it, j + 3])

    @functools.partial(loop, 0, 8)
    def _(j):
        for it in (0, 1):
            sent(other.at[0, 0], c_send.at[it, j])

            @pl.when(j > 0)
            def _():
                sent(other.at[0, 0], o_send.at[it, j - 1])


def hand_over(res_in, new_in, res_out, new_out):
    res_out[...] = res_in[...]
    new_out[...] = new_in[...]


def body(samples, targets, centres, coefficients):
    dma = pltpu.SemaphoreType.DMA
    vmem = pltpu.VMEM
    res_t, new_t = pl.pallas_call(
        step_kernel,
        out_shape=(jax.ShapeDtypeStruct((64, 512), f32), jax.ShapeDtypeStruct((64, 128), f32)),
        in_specs=[pl.BlockSpec(memory_space=pl.ANY)] * 4,
        out_specs=[pl.BlockSpec(memory_space=vmem)] * 2,
        scratch_shapes=[
            vmem((2048, 512), f32), vmem((64, 2048), f32), vmem((2, 512, 512), f32), vmem((64, 512), f32),
            vmem((8, 2, 128, 512), f32),
            vmem((2048, 1536), bf16), vmem((2048, 128), f32), vmem((8, 2048), f32),
            vmem((1024, 1536), bf16), vmem((1024, 128), f32), vmem((256, 1536), bf16), vmem((8, 256), f32),
            vmem((2048, 128), bf16),
            vmem((1024, 2048), bf16), vmem((1024, 2048), bf16), vmem((2048, 2048), bf16), vmem((2048, 2048), bf16),
            vmem((1024, 128), f32), vmem((2, 64, 512), f32), vmem((15, 8, 512), f32), vmem((2, 64, 512), f32),
            vmem((4, 64, 512), f32), vmem((3, SUM_TOP, 512), f32), vmem((SUM_TOP, 512), f32), vmem((3, SUM_TOP, 128), f32),
            vmem((3, 4, 64 - SUM_TOP, 128), f32), vmem((4, 64 - SUM_TOP, 128), f32), vmem((3, 64 - SUM_TOP, 128), f32),
            vmem((2, 4, 72, 512), f32), vmem((2, 72, 2048), f32), vmem((2, 8, 72, 128), f32), vmem((2, 8, 72, 128), f32),
            vmem((2, 7, 72, 128), f32), vmem((128, 1024), bf16), vmem((144, 512), bf16),
            dma((36,)), dma((4,)), dma((4,)), dma((8,)), dma((8,)), dma((8,)), dma((8,)), dma((4,)), dma((4,)),
            dma((15,)), dma((15,)), dma((15,)), dma((15,)),
            dma((3,)), dma((3,)), dma((3,)), dma((3,)), dma((3,)), dma((3,)), dma((3,)), dma((3,)),
            dma((2, 6)), dma((2, 6)), dma((2, 6)), dma((2, 6)),
            dma((2, 8)), dma((2, 8)), dma((2, 7)), dma((2, 7)),
        ],
        compiler_params=pltpu.CompilerParams(
            collective_id=0, has_side_effects=True, vmem_limit_bytes=63 * 2**20
        ),
    )(samples, targets.T, centres, coefficients.T)
    res_t, new_t = pl.pallas_call(
        hand_over,
        out_shape=(jax.ShapeDtypeStruct((64, 512), f32), jax.ShapeDtypeStruct((64, 128), f32)),
        in_specs=[pl.BlockSpec(memory_space=vmem)] * 2,
        out_specs=[pl.BlockSpec(memory_space=vmem)] * 2,
    )(res_t, new_t)
    return res_t.T, new_t.T


def solution(mesh):
    return jax.shard_map(
        body,
        mesh=mesh,
        in_specs=(P("dp", None), P("dp", None), P("centre", None), P("centre", None)),
        out_specs=(P("dp", None), P(("centre", "dp"), None)),
        check_vma=False,
    )
```

```python
import functools
import math

import jax
import jax.numpy as jnp
from jax import lax
from jax.experimental import pallas as pl
from jax.experimental.pallas import tpu as pltpu
from jax.sharding import PartitionSpec as P

MESH = pl.DeviceIdType.MESH
f32, bf16 = jnp.float32, jnp.bfloat16
NT = (((1,), (1,)), ((), ()))

SOFTENING = 0.01
KERNEL_SCALE = 0.2
LEARNING_RATE = 4.0
SCALE_SQ = (math.log2(math.e) / KERNEL_SCALE) ** 2
EPS = SOFTENING * SCALE_SQ

PAIRS = ((0, 0), (1, 0), (3, 0), (2, 0), (0, 1), (1, 1), (3, 1), (2, 1))
PLACE = {pair: at for at, pair in enumerate(PAIRS)}
FIRST_ROWS = ((1, 0), (3, 0), (0, 1))
LATER_ROWS = ((1, 1), (3, 1))
SUM_TOP = 40
TOP = 48


def halves(x):
    hi = x.astype(bf16)
    lo = (x - hi.astype(f32)).astype(bf16)
    return hi, lo


def kernel_of(z):
    z = jnp.maximum(z, EPS)
    return jnp.exp2(-(z * lax.rsqrt(z)))


def lanes(x, times):
    return jnp.concatenate([x] * times, axis=1)


def near_first(t):
    return t + t // 2 - 2 * (t // 3)


def loop(start, stop, f):
    def step(i, _):
        f(i)
        return 0

    lax.fori_loop(start, stop, step, 0)


def step_kernel(
    samples, targets, centres, coefs, res_out, new_out,
    cen, cof, smp, tgt, rows,
    c3, ccol, crow, s3, scol, r3, rrow, cof2,
    kh, kl, th, tl,
    pacc, pred, pred_in, res,
    gpart, g_y, gsum, g_z, h_z, hsum, h_y,
    whole, part, other, summed, arrived, lhs_r, lhs_u,
    loc_sem, smp_send, smp_recv, row_send, row_recv, fwd_send, fwd_recv, rel_send, rel_recv,
    p_send, p_recv, q_send, q_recv,
    gy_send, gy_recv, gz_send, gz_recv, hz_send, hz_recv, hy_send, hy_recv,
    a_send, a_recv, b_send, b_recv, c_send, c_recv, o_send, o_recv,
):
    n = 128
    d, c = lax.axis_index("dp"), lax.axis_index("centre")
    core, zh, y = d % 2, (d // 2) % 4, d // 8
    x, zl = c // 2, c % 2
    sib = d + 1 - 2 * core
    mine = pl.ds(pl.multiple_of(c * 8, 8), 8)
    own_rows = pl.ds(pl.multiple_of(d * n, n), n)
    sib_rows = pl.ds(pl.multiple_of(sib * n, n), n)

    def at_y(j):
        return (((y + j) % 4 * 4 + zh) * 2 + core, c)

    def at_z(j):
        return ((y * 4 + (zh + j) % 4) * 2 + core, c)

    def centre_of(dx, dz):
        return (x + dx) % 4 * 2 + (zl + dz) % 2

    def remote(src, dst, send, recv, to):
        return pltpu.make_async_remote_copy(
            src_ref=src, dst_ref=dst, send_sem=send, recv_sem=recv, device_id=to, device_id_type=MESH
        )

    def got(like, sem):
        remote(like, like, sem, sem, (sib, c)).wait_recv()

    def sent(like, sem):
        remote(like, like, sem, sem, (sib, c)).wait_send()

    def block_loads(b):
        owner = ((y + b // 4) % 4 * 4 + (zh + b % 4) % 4) * 2 + core
        at = pl.ds(pl.multiple_of(owner * n, n), n)
        to = pl.ds(pl.multiple_of(b * n, n), n)
        return (
            pltpu.make_async_copy(centres.at[at], cen.at[to], loc_sem.at[4 + b]),
            pltpu.make_async_copy(coefs.at[:, at], cof.at[:, to], loc_sem.at[20 + b]),
        )

    smp_load = pltpu.make_async_copy(samples, smp.at[0], loc_sem.at[0])
    late_loads = (
        pltpu.make_async_copy(targets, tgt, loc_sem.at[1]),
        pltpu.make_async_copy(centres.at[own_rows], rows.at[0, 0], loc_sem.at[2]),
        pltpu.make_async_copy(centres.at[sib_rows], rows.at[0, 1], loc_sem.at[3]),
    )
    smp_load.start()

    @functools.partial(loop, 0, 16)
    def _(b):
        for copy in block_loads(b):
            copy.start()

    for copy in late_loads:
        copy.start()

    barrier = pltpu.get_barrier_semaphore()
    partners = [(sib, c)] + [at_y(j) for j in (1, 2, 3)] + [at_z(j) for j in (1, 2, 3)]
    for dx, dz in PAIRS[1:]:
        partners += [(d, centre_of(dx, dz)), (sib, centre_of(dx, dz))]
    for to in partners:
        pl.semaphore_signal(barrier, inc=1, device_id=to, device_id_type=MESH)

    def send_rows(pairs):
        for dx, dz in pairs:
            j = PLACE[((4 - dx) % 4, dz)]
            remote(
                cen.at[pl.ds(0, n)], rows.at[j, 0], row_send.at[PLACE[(dx, dz)]], row_recv.at[j], (d, centre_of(dx, dz))
            ).start()

    def relay_rows(dz):
        far = PLACE[(2, dz)]
        for i, (back, on) in enumerate(((1, 3), (3, 1))):
            half = pl.ds(i * 64, 64)
            remote(
                rows.at[PLACE[(back, dz)], 0, half], rows.at[far, 0, half],
                rel_send.at[dz * 2 + i], rel_recv.at[dz * 2 + i], (d, centre_of(on, 0)),
            ).start()

    def await_relayed(dz):
        for i in (0, 1):
            got(rows.at[PLACE[(2, dz)], 0, pl.ds(i * 64, 64)], rel_recv.at[dz * 2 + i])

    def forward_rows(j):
        remote(rows.at[j, 0], rows.at[j, 1], fwd_send.at[j], fwd_recv.at[j], (sib, c)).start()

    def pass_on(pairs, dz):
        for pair in pairs:
            got(rows.at[PLACE[pair], 0], row_recv.at[PLACE[pair]])
        relay_rows(dz)
        for pair in pairs:
            forward_rows(PLACE[pair])

    def norm_of(v):
        total = jnp.sum(v * v, axis=1, keepdims=True) * SCALE_SQ
        return jnp.broadcast_to(total, (n, n))

    def prepare_samples(half):
        @functools.partial(loop, 0, 4)
        def _(i):
            at = pl.ds(pl.multiple_of(i * n, n), n)
            to = pl.ds(pl.multiple_of(half * 512 + i * n, n), n)
            v = smp[half, at, :]
            hi, lo = halves(v * (-2.0 * SCALE_SQ))
            s3[to, 0:512] = hi
            s3[to, 512:1024] = hi
            s3[to, 1024:1536] = lo
            scol[to, :] = norm_of(v) + EPS

    smp_load.wait()
    prepare_samples(0)

    @functools.partial(loop, 0, 16)
    def _(b):
        for copy in block_loads(b):
            copy.wait()
        at = pl.ds(pl.multiple_of(b * n, n), n)
        v = cen[at, :]
        hi, lo = halves(v)
        c3[at, 0:512] = hi
        c3[at, 512:1024] = lo
        c3[at, 1024:1536] = hi
        norms = norm_of(v)
        ccol[at, :] = norms + EPS
        crow[:, at] = norms.T[0:8, :]
        w = cof[:, at]
        whi = w.astype(bf16).astype(f32)
        cof2[at, :] = jnp.concatenate([whi, w - whi], axis=0).T.astype(bf16)

    def member(s):
        dx, dz, kk = s // 4, s // 2 % 2, s % 2
        return centre_of(dx, dz), d + kk * (sib - d), kk

    def send_predictions(kk):
        both = pacc[kk * 512 : kk * 512 + 512, :].T
        pred[kk] = both[0:64] + both[64:128]

        @functools.partial(loop, 0, 8)
        def _(t):
            s = (t + 4) % 8 * 2 + kk
            to, at_d, _ = member(s)

            @pl.when(s > 0)
            def _():
                remote(
                    pred.at[kk, pl.ds(pl.multiple_of(to * 8, 8), 8)],
                    pred_in.at[s - 1], p_send.at[s - 1], p_recv.at[s - 1], (at_d, to),
                ).start()

    tn = 1024
    pacc[...] = jnp.zeros_like(pacc)

    @functools.partial(loop, 0, 4)
    def _(i):
        @pl.when(i == 1)
        def _():
            pl.semaphore_wait(barrier, len(partners))
            for k in range(4):
                at = pl.ds(k * n, n)
                remote(smp.at[0, at], smp.at[1, at], smp_send.at[k], smp_recv.at[k], (sib, c)).start()
            send_rows(FIRST_ROWS)

        @pl.when(i == 2)
        def _():
            for k in range(4):
                got(smp.at[1, pl.ds(k * n, n)], smp_recv.at[k])
            prepare_samples(1)
            send_predictions(0)

        these = pl.ds(pl.multiple_of(i // 2 * 512, 512), 512)
        at = pl.ds(pl.multiple_of(i % 2 * tn, tn), tn)
        cross = lax.dot_general(s3[these, :], c3[at, :], NT, preferred_element_type=f32)
        value = kernel_of(cross + lanes(scol[these, :], tn // n) + crow[0:1, at])
        hi, lo = halves(value)
        kh[these, at] = hi
        kl[these, at] = lo
        w = cof2[at, :]
        pacc[these, :] += jnp.dot(hi, w, preferred_element_type=f32) + jnp.dot(lo, w, preferred_element_type=f32)

    send_predictions(1)
    for copy in late_loads:
        copy.wait()
    pass_on(FIRST_ROWS, 0)

    def residuals():
        loop(0, 15, lambda s: got(pred_in.at[s], p_recv.at[s]))
        total = pred[0, mine, :] - tgt[mine, :]
        for s in range(15):
            total += pred_in[s]
        res[0, mine, :] = total

        @functools.partial(loop, 0, 16)
        def _(t):
            s = (t + 8) % 16
            to, at_d, kk = member(s)

            @pl.when(s > 0)
            def _():
                remote(res.at[0, mine], res.at[kk, mine], q_send.at[s - 1], q_recv.at[s - 1], (at_d, to)).start()

        for dx in (1, 3):
            j = PLACE[(4 - dx, 1)]
            remote(
                rows.at[PLACE[(0, 1)], 0], rows.at[j, 0], row_send.at[PLACE[(dx, 1)]], row_recv.at[j],
                (d, centre_of(dx, 0)),
            ).start()
        got(rows.at[1, 0], fwd_recv.at[1])
        got(rows.at[2, 0], fwd_recv.at[2])

    top, low = pl.ds(0, SUM_TOP), pl.ds(SUM_TOP, 64 - SUM_TOP)

    def gradients():
        loop(0, 15, lambda s: got(res.at[0, pl.ds(0, 8)], q_recv.at[s]))
        for kk in (0, 1):
            hi, lo = halves(res[kk])
            lhs_r[0:64, kk * 512 : kk * 512 + 512] = lo
            lhs_r[64:128, kk * 512 : kk * 512 + 512] = hi

        @functools.partial(loop, 0, 4)
        def _(t):
            dy = 2 - t + 3 * (t // 2) - 2 * (t // 3)
            at = pl.ds(pl.multiple_of(dy * 512, 512), 512)
            a = jnp.dot(lhs_r[...], kh[:, at], preferred_element_type=f32)
            b = jnp.dot(lhs_r[64:128, :], kl[:, at], preferred_element_type=f32)
            gpart[dy] = a[0:64] + a[64:128] + b

            @pl.when(t < 3)
            def _():
                remote(gpart.at[dy, top], g_y.at[dy - 1], gy_send.at[dy - 1], gy_recv.at[dy - 1], at_y(dy)).start()

        for j in (2, 1, 3):
            remote(
                gpart.at[:, low, pl.ds(j * n, n)], h_z.at[j - 1], hz_send.at[j - 1], hz_recv.at[j - 1], at_z(j)
            ).start()
        res_out[...] = res[0]
        got(rows.at[3, 0], fwd_recv.at[3])
        got(rows.at[4, 0], fwd_recv.at[4])

    first, rests = pl.ds(0, TOP), (pl.ds(TOP, 64 - TOP), pl.ds(TOP, 72 - TOP))
    start = pl.ds(0, n)

    def spread_first(it):
        rest = rests[it]
        for j in (2, 1, 3):
            to = 4 - j
            remote(
                whole.at[it, 0, first, start], whole.at[it, 0, first, pl.ds(to * n, n)],
                a_send.at[it, j - 1], a_recv.at[it, j - 1], at_z(j),
            ).start()
            remote(
                whole.at[it, 0, rest, start], whole.at[it, to, rest, start],
                a_send.at[it, j + 2], a_recv.at[it, j + 2], at_y(j),
            ).start()

    def spread_more(it):
        rest = rests[it]
        for j in (1, 2, 3):
            got(whole.at[it, 0, rest, start], a_recv.at[it, j + 2])
        for j in (2, 1, 3):
            to = 4 - j
            remote(
                whole.at[it, :, rest, start], whole.at[it, :, rest, pl.ds(to * n, n)],
                b_send.at[it, j - 1], b_recv.at[it, j - 1], at_z(j),
            ).start()
        for j in (1, 2, 3):
            got(whole.at[it, 0, first, start], a_recv.at[it, j - 1])
        for j in (2, 1, 3):
            remote(
                whole.at[it, 0, first], whole.at[it, 4 - j, first],
                b_send.at[it, j + 2], b_recv.at[it, j + 2], at_y(j),
            ).start()

    def sum_gradients():
        for j in range(3):
            got(g_y.at[j], gy_recv.at[j])
        gsum[...] = gpart[0, 0:SUM_TOP] + g_y[0] + g_y[1] + g_y[2]
        for j in (2, 1, 3):
            remote(
                gsum.at[:, pl.ds(j * n, n)], g_z.at[j - 1], gz_send.at[j - 1], gz_recv.at[j - 1], at_z(j)
            ).start()
        for j in range(3):
            got(h_z.at[j], hz_recv.at[j])
        hsum[...] = gpart[:, SUM_TOP:64, 0:n] + h_z[0] + h_z[1] + h_z[2]
        for j in (2, 1, 3):
            remote(hsum.at[j], h_y.at[j - 1], hy_send.at[j - 1], hy_recv.at[j - 1], at_y(j)).start()
        for j in range(3):
            got(g_z.at[j], gz_recv.at[j])
            got(h_y.at[j], hy_recv.at[j])
        whole[0, 0, 0:SUM_TOP, 0:n] = gsum[:, 0:n] + g_z[0] + g_z[1] + g_z[2]
        whole[0, 0, SUM_TOP:64, 0:n] = hsum[0] + h_y[0] + h_y[1] + h_y[2]
        spread_first(0)
        got(rows.at[5, 0], fwd_recv.at[5])

    def spread_gradients():
        spread_more(0)
        await_relayed(1)
        forward_rows(7)
        got(rows.at[6, 0], fwd_recv.at[6])


    @functools.partial(loop, 0, 8)
    def _(j):
        for kk in (0, 1):
            v = rows[j, kk]
            hi, lo = halves(v * (-2.0 * SCALE_SQ))
            to = slice(kk * n, kk * n + n)
            r3[to, 0:512] = hi
            r3[to, 512:1024] = hi
            r3[to, 1024:1536] = lo
            rrow[:, to] = norm_of(v).T[0:8, :]
        cols = pl.ds(pl.multiple_of(j * 256, 256), 256)

        cross = lax.dot_general(c3[...], r3[...], NT, preferred_element_type=f32)
        hi, lo = halves(kernel_of(cross + lanes(ccol[...], 2) + rrow[0:1, :]))
        th[:, cols] = hi
        tl[:, cols] = lo

        pl.when(j == 0)(residuals)
        pl.when(j == 2)(gradients)

        @pl.when(j == 1)
        def _():
            await_relayed(0)
            forward_rows(PLACE[(2, 0)])

        @pl.when(j == 3)
        def _():
            pass_on(LATER_ROWS, 1)

        pl.when(j == 4)(sum_gradients)
        pl.when(j == 5)(spread_gradients)

        @pl.when(j == 6)
        def _():
            got(rows.at[7, 0], fwd_recv.at[7])

    lhs_u[128:144, :] = jnp.ones((16, 512), bf16)
    part[...] = jnp.zeros_like(part)

    @functools.partial(loop, 0, 2)
    def _(it):
        @functools.partial(loop, 0, 4)
        def _(t):
            dy = near_first(t)

            for turn in (0, 1):

                @pl.when((t == 0) & (it == turn))
                def _():
                    for j in range(3):
                        got(whole.at[turn, :, rests[turn], start], b_recv.at[turn, j])

            @pl.when(t > 0)
            def _():
                got(whole.at[0, 0, first], b_recv.at[it, 6 - dy])

            hi, lo = halves(whole[it, dy, 0:64, :])
            lhs_u[0:64, :] = lo
            lhs_u[64:128, :] = hi
            k = pl.ds(pl.multiple_of(dy * 512, 512), 512)

            @functools.partial(loop, 0, 2)
            def _(back):
                i = 1 - back
                at = pl.ds(pl.multiple_of(i * 1024, 1024), 1024)
                a = jnp.dot(lhs_u[...], th[k, at], preferred_element_type=f32)
                b = jnp.dot(lhs_u[64:144, :], tl[k, at], preferred_element_type=f32)
                part[it, 0:64, at] += a[0:64] + a[64:128] + b[0:64]
                part[it, 64:72, at] += a[128:136] + b[64:72]

                @pl.when(t == 3)
                def _():
                    @pl.when(it == 1)
                    def _():
                        largest = whole[1, 0, 64:72, 0:n]
                        for e in range(1, 16):
                            largest = jnp.maximum(largest, whole[1, e // 4, 64:72, e % 4 * n : e % 4 * n + n])
                        largest = lanes(largest, 8)
                        part[1, 64:72, at] = largest

                    for j in (4 * i + 3, 4 * i + 2, 4 * i + 1, 4 * i):
                        theirs = pl.ds(pl.multiple_of((2 * j + 1) * n, n), n)
                        remote(
                            part.at[it, :, theirs], other.at[it, j], c_send.at[it, j], c_recv.at[it, j], (sib, c)
                        ).start()

        def added(a, b):
            return jnp.concatenate([a[0:64] + b[0:64], jnp.where(it == 1, jnp.maximum(a[64:72], b[64:72]), a[64:72] + b[64:72])])

        @functools.partial(loop, 0, 8)
        def _(back):
            j = 7 - back
            got(other.at[0, 0], c_recv.at[it, j])
            ours = pl.ds(pl.multiple_of(2 * j * n, n), n)
            summed[it, j] = added(part[it, :, ours], other[it, j])

            @pl.when(j > 0)
            def _():
                to = centre_of(near_first(j % 4), j // 4)
                remote(
                    summed.at[it, j], arrived.at[it, j - 1], o_send.at[it, j - 1], o_recv.at[it, j - 1], (d, to)
                ).start()

        loop(0, 7, lambda s: got(arrived.at[0, 0], o_recv.at[it, s]))
        total = summed[it, 0]
        for s in range(7):
            total = added(total, arrived[it, s])

        @pl.when(it == 0)
        def _():
            whole[1, 0, 0:64, 0:n] = total[0:64]
            whole[1, 0, 64:72, 0:n] = jnp.broadcast_to(jnp.max(total[64:72], axis=1, keepdims=True), (8, n))
            spread_first(1)
            spread_more(1)

        @pl.when(it == 1)
        def _():
            size = jnp.concatenate([1.0 / total[64:72]] * 8, axis=0)
            once, grad = whole[1, 0, 0:64, 0:n], whole[0, 0, 0:64, 0:n]
            theta = size * (3.0 * grad - size * (3.0 * once - size * total[0:64]))
            new_out[...] = cof[:, 0:n] - LEARNING_RATE * theta

    for i in range(4):
        sent(smp.at[0, pl.ds(0, n)], smp_send.at[i])
        sent(rows.at[0, 0, pl.ds(0, 64)], rel_send.at[i])
    for pair in FIRST_ROWS + LATER_ROWS:
        sent(rows.at[0, 0], row_send.at[PLACE[pair]])
    loop(1, 8, lambda j: sent(rows.at[0, 0], fwd_send.at[j]))

    @functools.partial(loop, 0, 15)
    def _(s):
        sent(pred_in.at[0], p_send.at[s])
        sent(pred_in.at[0], q_send.at[s])

    @functools.partial(loop, 0, 3)
    def _(j):
        sent(g_y.at[0], gy_send.at[j])
        sent(g_z.at[0], gz_send.at[j])
        sent(h_z.at[0], hz_send.at[j])
        sent(h_y.at[0], hy_send.at[j])
        for it in (0, 1):
            sent(whole.at[0, 0, first, start], a_send.at[it, j])
            sent(whole.at[0, 0, rests[it], start], a_send.at[it, j + 3])
            sent(whole.at[0, :, rests[it], start], b_send.at[it, j])
            sent(whole.at[0, 0, first], b_send.at[it, j + 3])

    @functools.partial(loop, 0, 8)
    def _(j):
        for it in (0, 1):
            sent(other.at[0, 0], c_send.at[it, j])

            @pl.when(j > 0)
            def _():
                sent(other.at[0, 0], o_send.at[it, j - 1])


def hand_over(res_in, new_in, res_out, new_out):
    res_out[...] = res_in[...]
    new_out[...] = new_in[...]


def body(samples, targets, centres, coefficients):
    dma = pltpu.SemaphoreType.DMA
    vmem = pltpu.VMEM
    res_t, new_t = pl.pallas_call(
        step_kernel,
        out_shape=(jax.ShapeDtypeStruct((64, 512), f32), jax.ShapeDtypeStruct((64, 128), f32)),
        in_specs=[pl.BlockSpec(memory_space=pl.ANY)] * 4,
        out_specs=[pl.BlockSpec(memory_space=vmem)] * 2,
        scratch_shapes=[
            vmem((2048, 512), f32), vmem((64, 2048), f32), vmem((2, 512, 512), f32), vmem((64, 512), f32),
            vmem((8, 2, 128, 512), f32),
            vmem((2048, 1536), bf16), vmem((2048, 128), f32), vmem((8, 2048), f32),
            vmem((1024, 1536), bf16), vmem((1024, 128), f32), vmem((256, 1536), bf16), vmem((8, 256), f32),
            vmem((2048, 128), bf16),
            vmem((1024, 2048), bf16), vmem((1024, 2048), bf16), vmem((2048, 2048), bf16), vmem((2048, 2048), bf16),
            vmem((1024, 128), f32), vmem((2, 64, 512), f32), vmem((15, 8, 512), f32), vmem((2, 64, 512), f32),
            vmem((4, 64, 512), f32), vmem((3, SUM_TOP, 512), f32), vmem((SUM_TOP, 512), f32), vmem((3, SUM_TOP, 128), f32),
            vmem((3, 4, 64 - SUM_TOP, 128), f32), vmem((4, 64 - SUM_TOP, 128), f32), vmem((3, 64 - SUM_TOP, 128), f32),
            vmem((2, 4, 72, 512), f32), vmem((2, 72, 2048), f32), vmem((2, 8, 72, 128), f32), vmem((2, 8, 72, 128), f32),
            vmem((2, 7, 72, 128), f32), vmem((128, 1024), bf16), vmem((144, 512), bf16),
            dma((36,)), dma((4,)), dma((4,)), dma((8,)), dma((8,)), dma((8,)), dma((8,)), dma((4,)), dma((4,)),
            dma((15,)), dma((15,)), dma((15,)), dma((15,)),
            dma((3,)), dma((3,)), dma((3,)), dma((3,)), dma((3,)), dma((3,)), dma((3,)), dma((3,)),
            dma((2, 6)), dma((2, 6)), dma((2, 6)), dma((2, 6)),
            dma((2, 8)), dma((2, 8)), dma((2, 7)), dma((2, 7)),
        ],
        compiler_params=pltpu.CompilerParams(
            collective_id=0, has_side_effects=True, vmem_limit_bytes=63 * 2**20
        ),
    )(samples, targets.T, centres, coefficients.T)
    res_t, new_t = pl.pallas_call(
        hand_over,
        out_shape=(jax.ShapeDtypeStruct((64, 512), f32), jax.ShapeDtypeStruct((64, 128), f32)),
        in_specs=[pl.BlockSpec(memory_space=vmem)] * 2,
        out_specs=[pl.BlockSpec(memory_space=vmem)] * 2,
    )(res_t, new_t)
    return res_t.T, new_t.T


def solution(mesh):
    return jax.shard_map(
        body,
        mesh=mesh,
        in_specs=(P("dp", None), P("dp", None), P("centre", None), P("centre", None)),
        out_specs=(P("dp", None), P(("centre", "dp"), None)),
        check_vma=False,
    )
```
